768 devices in a mesh: rep: 12 (over z), sp: 64 (over x, y, core).
Axes of the slice: x: 4, y: 8, z: 12, core: 2. Of those that a mesh axis runs over, the one named last changes fastest.
Arguments:
- inputs: bfloat16 [12, 64, 16, 4096], P('rep', 'sp'), may hold values from -6 to 6
- preact: bfloat16 [12, 64, 16, 4096], P('rep', 'sp'), may hold values from -6 to 6
- grad_out: bfloat16 [12, 64, 16, 4096], P('rep', 'sp'), may hold values from -20 to 20
- weight: bfloat16 [3, 3, 3, 64, 64], replicated, may hold values from -0.15625 to 0.15625
Outputs:
- input_grad: bfloat16 [12, 64, 16, 4096], P('rep', 'sp')
- weight_grad: float32 [3, 3, 3, 64, 64], replicated
- bias_grad: float32 [64], replicated
The draws below stay inside these ranges and needn't reach their ends.
All inputs are finite; a program needn't handle non-finite values.
Results may differ from the reference program's by a relative error of at most 0.001.
Values may be sent and summed in bfloat16 or wider, within the bound.
No kernel may reach another device: no remote copies, remote signals or barrier semaphores. Data moves between devices by JAX's collectives and lax.ppermute only.
A program may use at most 32 MiB of HBM per device.

```python
import jax
import jax.numpy as jnp
from jax import lax

CH = 64
WIDTH = 64
HEIGHT = 16
BATCH = 12
DEPTH = 64


def draw_grad_out(key, part):
    shape = (BATCH, DEPTH, HEIGHT, WIDTH * CH)
    first = jax.random.fold_in(key, 0)
    base = jax.random.normal(first, shape, jnp.float32)
    position = jnp.arange(DEPTH, dtype=jnp.float32) / max(DEPTH - 1, 1)
    factor = jnp.exp(position * jnp.log(3.0))
    return jnp.clip(base * factor[None, :, None, None], -20.0, 20.0).astype(jnp.bfloat16)


def levels(stream_key, dims, cuts, smallest, high):
    loudness, own = 1.0, jax.random.fold_in(stream_key, 6)
    for axis_at, blocks in cuts:
        heights = jnp.exp(jax.random.uniform(jax.random.fold_in(own, axis_at), (blocks,), jnp.float32, smallest / len(cuts), high / len(cuts)))
        loudness = loudness * jnp.repeat(heights, dims[axis_at] // blocks).reshape([-1 if axis == axis_at else 1 for axis in range(len(dims))])
    return loudness


def centred(own_key, dims, spread, most, shards=(), kind=jnp.bfloat16):
    level = levels(own_key, dims, shards, -0.22, 0.18) if shards else 1.0
    array = jax.random.normal(own_key, dims, jnp.float32) * spread * level
    return jnp.minimum(jnp.maximum(array, -most), most).astype(kind)


def setup_inputs(seed: int = 0) -> dict:
    seeds = jax.random.split(jax.random.key(seed), 5)
    inputs = centred(seeds[0], (BATCH, DEPTH, HEIGHT, WIDTH * CH), 1.0, 6.0, ((0, 12), (1, 64)))
    preact = centred(seeds[1], (BATCH, DEPTH, HEIGHT, WIDTH * CH), 1.0, 6.0, ((0, 12), (1, 64)))
    grad_out = draw_grad_out(jax.random.fold_in(seeds[4], 71), 0)
    weight = centred(seeds[3], (3, 3, 3, CH, CH), (27 * CH) ** -0.5, 0.15625)
    return {"inputs": inputs, "preact": preact, "grad_out": grad_out, "weight": weight}


def unfold(volume, channels):
    samples, planes, height, packed = volume.shape
    cells = packed // channels
    shaped = volume.reshape(samples, planes, height, cells, channels)
    padded = jnp.pad(shaped, ((0, 0), (0, 0), (1, 1), (1, 1), (0, 0)))
    pieces = []
    for tap_h in range(3):
        for tap_w in range(3):
            pieces.append(padded[:, :, tap_h:tap_h + height, tap_w:tap_w + cells, :])
    stacked = jnp.concatenate(pieces, axis=4)
    return stacked.reshape(-1, 9 * channels)


def reference(inputs, preact, grad_out, weight):
    channels = weight.shape[3]
    flipped = jnp.transpose(weight[::-1, ::-1, ::-1], (0, 1, 2, 4, 3))

    def one_sample(operands):
        x_one, z_one, dy_one = operands
        x_one = x_one[None]
        grad_masked = jnp.where(z_one[None] > 0, dy_one[None], jnp.zeros_like(dy_one[None]))
        planes = x_one.shape[1]
        grad_padded = jnp.pad(grad_masked, ((0, 0), (1, 1), (0, 0), (0, 0)))
        input_padded = jnp.pad(x_one, ((0, 0), (1, 1), (0, 0), (0, 0)))
        grad_flat = grad_masked.reshape(-1, channels)
        totals = jnp.zeros((grad_flat.shape[0], channels), jnp.float32)
        kernel_rows = []
        for depth_tap in range(3):
            grad_cols = unfold(grad_padded[:, depth_tap:depth_tap + planes], channels)
            totals = totals + jnp.dot(grad_cols, flipped[depth_tap].reshape(9 * channels, channels), preferred_element_type=jnp.float32)
            input_cols = unfold(input_padded[:, depth_tap:depth_tap + planes], channels)
            part = lax.dot_general(input_cols, grad_flat, (((0,), (0,)), ((), ())), preferred_element_type=jnp.float32)
            kernel_rows.append(part.reshape(3, 3, channels, channels))
        dx_one = totals.reshape(grad_masked.shape[1:]).astype(jnp.bfloat16)
        dw_one = jnp.stack(kernel_rows, axis=0)
        db_one = jnp.sum(grad_flat.astype(jnp.float32), axis=0)
        return dx_one, dw_one, db_one

    input_grad, kernel_each, bias_each = lax.map(one_sample, (inputs, preact, grad_out))
    scale = 1.0 / (BATCH * DEPTH * HEIGHT * WIDTH) ** 0.5
    weight_grad = jnp.sum(kernel_each, axis=0) * scale
    bias_grad = jnp.sum(bias_each, axis=0) * scale
    return input_grad, weight_grad, bias_grad
```

```python
import jax
import jax.numpy as jnp
from jax import lax
from jax.experimental import pallas as pl
from jax.experimental.pallas import tpu as pltpu
from jax.sharding import PartitionSpec as P


CH = 64
LANES = 2 * CH
CHUNK = 14
SMALL = pltpu.CompilerParams(vmem_limit_bytes=16 * 1024 * 1024)


def mask_kernel(preact_ref, grad_ref, x_ref, own_ref, pack_ref, z_ref, dy_ref, sems):
    height = own_ref.shape[0]
    loads = (
        pltpu.make_async_copy(preact_ref, z_ref, sems.at[0]),
        pltpu.make_async_copy(grad_ref, dy_ref, sems.at[1]),
        pltpu.make_async_copy(x_ref, pack_ref.at[height:], sems.at[2]),
    )
    for load in loads:
        load.start()
    loads[0].wait()
    loads[1].wait()
    own = jnp.where(z_ref[...] > 0, dy_ref[...], jnp.zeros_like(dy_ref))
    own_ref[...] = own
    pack_ref[0:height, :] = own
    loads[2].wait()


def inputs_kernel(pair_ref, xt_ref):
    height, packed = pair_ref.shape[0] // 2, pair_ref.shape[1]
    x_ref = pair_ref.at[height:]
    pairs = packed // LANES
    rows = pairs * height
    x = jnp.concatenate([x_ref[:, LANES * j : LANES * (j + 1)] for j in range(pairs)], axis=0)
    xt = jnp.transpose(x.astype(jnp.float32))
    h = lax.broadcasted_iota(jnp.int32, (LANES, rows), 1) % height
    xt_ref[0:LANES, :] = jnp.where(h == 0, 0.0, pltpu.roll(xt, 1, 1)).astype(jnp.bfloat16)
    xt_ref[LANES : 2 * LANES, :] = xt.astype(jnp.bfloat16)
    xt_ref[2 * LANES :, :] = jnp.where(h == height - 1, 0.0, pltpu.roll(xt, rows - 1, 1)).astype(jnp.bfloat16)


def weights_kernel(core_ref, w_ref, wt_ref):
    core = core_ref[0]
    zero = jnp.zeros((CH, CH), jnp.bfloat16)
    for slot, od in enumerate((2 - 2 * core, 1, 2 * core)):
        for oh in range(3):
            t = 9 * od + 3 * oh
            before, here, after = w_ref[t], w_ref[t + 1], w_ref[t + 2]
            for parity in range(2):
                if parity == 0:
                    parts = (here, before, zero, after)
                else:
                    parts = (after, here, before, zero)
                r = (2 * oh + parity) * CH
                wt_ref[r : r + CH, 256 * slot : 256 * slot + LANES] = jnp.concatenate(parts[:2], axis=1)
                wt_ref[r : r + CH, 256 * slot + LANES : 256 * (slot + 1)] = jnp.concatenate(parts[2:], axis=1)


def kernel_gradient_kernel(core_ref, far_ref, own_ref, near_ref, xt_own_ref, xt_near_ref, dw_ref, g_ref):
    height, packed = own_ref.shape
    pairs = packed // LANES
    low = lax.broadcasted_iota(jnp.int32, (height, LANES), 1) < CH
    for slot, ref in enumerate((far_ref, own_ref, near_ref)):
        for j in range(pairs):
            at = slice(height * j, height * (j + 1))
            g_ref[at, 256 * slot : 256 * slot + LANES] = ref[0:height, LANES * j : LANES * (j + 1)]
            nothing = jnp.zeros((height, LANES), jnp.bfloat16)
            right = ref[0:height, LANES * (j + 1) : LANES * (j + 2)] if j + 1 < pairs else nothing
            left = ref[0:height, LANES * (j - 1) : LANES * j] if j > 0 else nothing
            g_ref[at, 256 * slot + LANES : 256 * (slot + 1)] = jnp.where(low, right, left)
    d = jnp.dot(xt_own_ref[...], g_ref[:, 0:512], preferred_element_type=jnp.float32)
    d = d + jnp.dot(xt_near_ref[...], g_ref[:, 256:768], preferred_element_type=jnp.float32)
    lo = lax.broadcasted_iota(jnp.int32, (CH, LANES), 1) < CH
    core_0 = jnp.full((CH, LANES), core_ref[0], jnp.int32) == 0

    def block(part, oh, parity, half):
        r = LANES * oh + CH * parity
        c = 256 * part + LANES * half
        return d[r : r + CH, c : c + LANES]

    def swap(v):
        return pltpu.roll(v, CH, 1)

    def two(part, oh):
        return block(part, oh, 0, 0) + jnp.where(lo, swap(block(part, oh, 1, 0)), swap(block(part, oh, 1, 1)))

    def low_one(part, oh):
        return block(part, oh, 1, 0) + swap(block(part, oh, 0, 1))

    def high_one(part, oh):
        return swap(block(part, oh, 1, 0)) + block(part, oh, 0, 1)

    total = jnp.sum(g_ref[:, 256:384].astype(jnp.float32) + g_ref[:, 512:640].astype(jnp.float32), axis=0, keepdims=True)
    first = lax.broadcasted_iota(jnp.int32, (CH, LANES), 0) == 0
    bias = jnp.where(first, jnp.broadcast_to(total + swap(total), (CH, LANES)), 0.0)
    blocks = (
        two(0, 0),
        two(0, 1),
        two(0, 2),
        jnp.where(lo, low_one(0, 0), high_one(0, 1)),
        jnp.where(lo, low_one(0, 2), jnp.where(core_0, high_one(1, 0), high_one(1, 2))),
        jnp.where(core_0, two(1, 0), two(1, 2)),
        jnp.where(core_0, two(1, 1), jnp.where(lo, low_one(1, 1), bias)),
    )
    for i, v in enumerate(blocks):
        dw_ref[CH * i : CH * (i + 1), :] = v


def input_gradient_kernel(g_ref, wt_ref, dx_ref):
    height, packed = dx_ref.shape
    pairs = packed // LANES
    rows = pairs * height
    y = lax.dot_general(
        g_ref[...], wt_ref[...], (((1,), (1,)), ((), ())), preferred_element_type=jnp.float32
    )
    h = lax.broadcasted_iota(jnp.int32, (rows, LANES), 0) % height
    up = jnp.where(h == height - 1, 0.0, pltpu.roll(y[:, :LANES], rows - 1, 0))
    down = jnp.where(h == 0, 0.0, pltpu.roll(y[:, 2 * LANES :], 1, 0))
    out = (y[:, LANES : 2 * LANES] + up + down).astype(jnp.bfloat16)
    for j in range(pairs):
        dx_ref[:, LANES * j : LANES * (j + 1)] = out[height * j : height * (j + 1), :]


def sum_kernel(parts_ref, out_ref, *, scale):
    group = 4 * CHUNK
    total = parts_ref[0:group, :]
    for i in range(1, parts_ref.shape[0] // group):
        total = total + parts_ref[group * i : group * (i + 1), :]
    s = (total[0:CHUNK] + total[CHUNK : 2 * CHUNK]) + (total[2 * CHUNK : 3 * CHUNK] + total[3 * CHUNK :])
    s = s * scale
    four = jnp.concatenate([s, s, s, s], axis=0)
    for i in range(out_ref.shape[0] // group):
        out_ref[group * i : group * (i + 1), :] = four


def unpack_kernel(core_ref, mine_ref, other_ref, weight_ref, bias_ref):
    core_0 = jnp.full((CH, LANES), core_ref[0], jnp.int32) == 0
    places = (
        ((19, 18), (22, 21), (25, 24), (20, 23), (26, 11), (10, 9), (13, 12)),
        ((1, 0), (4, 3), (7, 6), (2, 5), (8, 17), (16, 15), (14, None)),
    )
    for half, sides in enumerate(places):
        for i, (lower, upper) in enumerate(sides):
            a = mine_ref[CH * i : CH * (i + 1), :]
            b = other_ref[CH * i : CH * (i + 1), :]
            v = jnp.where(core_0, a, b) if half == 0 else jnp.where(core_0, b, a)
            weight_ref[lower] = v[:, :CH]
            if upper is None:
                bias_ref[...] = v[0:1, CH:]
            else:
                weight_ref[upper] = v[:, CH:]


def in_vmem(array):
    return pltpu.with_memory_space_constraint(array, pltpu.VMEM)


def in_hbm(array):
    return pltpu.with_memory_space_constraint(array, pltpu.HBM)


def sum_and_copy(parts, copies, scale):
    return pl.pallas_call(
        lambda p, o: sum_kernel(p, o, scale=scale),
        out_shape=pltpu.VMEM((copies * CHUNK, LANES), jnp.float32),
        compiler_params=SMALL,
    )(in_vmem(parts))


def exchange(rows, axis):
    return lax.all_to_all(rows.reshape(-1, 1, LANES), axis, 0, 0, tiled=True).reshape(-1, LANES)


def on_device(inputs, preact, grad_out, weight):
    chips = lax.axis_size("chip")
    slabs = chips * lax.axis_size("core")
    groups = lax.axis_size("rep")
    _, planes, height, packed = inputs.shape
    count = inputs.shape[0] * groups * planes * slabs * height * (packed // CH)
    scale = 1.0 / float(count) ** 0.5
    core = lax.axis_index("core").astype(jnp.int32).reshape(1)
    in_smem = pl.BlockSpec(memory_space=pltpu.SMEM)
    whole = pl.BlockSpec(memory_space=pltpu.VMEM)
    rows = height * packed // LANES
    own, pack = pl.pallas_call(
        mask_kernel,
        in_specs=[pl.BlockSpec(memory_space=pltpu.HBM)] * 3,
        out_shape=(
            pltpu.VMEM((height, packed), jnp.bfloat16),
            pltpu.VMEM((2 * height, packed), jnp.bfloat16),
        ),
        scratch_shapes=[pltpu.VMEM((height, packed), jnp.bfloat16)] * 2 + [pltpu.SemaphoreType.DMA((3,))],
        compiler_params=SMALL,
        name="mask",
    )(*(in_hbm(a.reshape(height, packed)) for a in (preact, grad_out, inputs)))
    swap = [(0, 1), (1, 0)]
    ends = range(1, slabs - 1, 2)
    far = lax.ppermute(own, ("chip", "core"), [(i, i + 1) for i in ends] + [(i + 1, i) for i in ends])
    near = in_vmem(lax.ppermute(pack, "core", swap))
    wt = pl.pallas_call(
        weights_kernel,
        in_specs=[in_smem, whole],
        out_shape=pltpu.VMEM((3 * LANES, 768), jnp.bfloat16),
        compiler_params=SMALL,
        name="weights",
    )(core, weight.reshape(27, CH, CH))

    def turned(pair):
        return pl.pallas_call(
            inputs_kernel,
            out_shape=pltpu.VMEM((3 * LANES, rows), jnp.bfloat16),
            compiler_params=SMALL,
            name="inputs",
        )(in_vmem(pair))

    dw, g = pl.pallas_call(
        kernel_gradient_kernel,
        in_specs=[in_smem] + [whole] * 5,
        out_shape=(
            pltpu.VMEM((chips * CHUNK, LANES), jnp.float32),
            pltpu.VMEM((rows, 768), jnp.bfloat16),
        ),
        compiler_params=SMALL,
        name="kernel_gradient",
    )(core, in_vmem(far), in_vmem(own), near, in_vmem(turned(pack)), in_vmem(turned(near)))
    dx = pl.pallas_call(
        input_gradient_kernel,
        out_shape=jax.ShapeDtypeStruct((height, packed), jnp.bfloat16),
        compiler_params=SMALL,
        name="input_gradient",
    )(in_vmem(g), in_vmem(wt))
    mine = sum_and_copy(exchange(dw, "chip"), groups, 1.0)
    total = sum_and_copy(exchange(mine, "rep"), chips, scale)
    gathered = exchange(total, "chip")
    other = lax.ppermute(gathered, "core", swap)
    weight_grad, bias_grad = pl.pallas_call(
        unpack_kernel,
        in_specs=[in_smem, whole, whole],
        out_shape=(
            jax.ShapeDtypeStruct((27, CH, CH), jnp.float32),
            jax.ShapeDtypeStruct((1, CH), jnp.float32),
        ),
        compiler_params=SMALL,
        name="unpack",
    )(core, in_vmem(gathered), in_vmem(other))
    return dx.reshape(inputs.shape), weight_grad.reshape(3, 3, 3, CH, CH), bias_grad.reshape(CH)


def solution(mesh):
    groups, slabs = mesh.devices.shape
    by_core = jax.sharding.Mesh(mesh.devices.reshape(groups, slabs // 2, 2), ("rep", "chip", "core"))
    split = P("rep", ("chip", "core"), None, None)
    return jax.shard_map(
        on_device,
        mesh=by_core,
        in_specs=(split, split, split, P()),
        out_specs=(split, P(), P()),
        check_vma=False,
    )
```

```python
import jax
import jax.numpy as jnp
from jax import lax
from jax.experimental import pallas as pl
from jax.experimental.pallas import tpu as pltpu
from jax.sharding import PartitionSpec as P


CH = 64
LANES = 2 * CH
SLOT = 16
CHUNK = 14
SMALL = pltpu.CompilerParams(vmem_limit_bytes=16 * 1024 * 1024)


def mask_kernel(preact_ref, grad_ref, x_ref, own_ref, pack_ref, z_ref, dy_ref, sems):
    height = own_ref.shape[0]
    loads = (
        pltpu.make_async_copy(preact_ref, z_ref, sems.at[0]),
        pltpu.make_async_copy(grad_ref, dy_ref, sems.at[1]),
        pltpu.make_async_copy(x_ref, pack_ref.at[height:], sems.at[2]),
    )
    for load in loads:
        load.start()
    loads[0].wait()
    loads[1].wait()
    own = jnp.where(z_ref[...] > 0, dy_ref[...], jnp.zeros_like(dy_ref))
    own_ref[...] = own
    pack_ref[0:height, :] = own
    loads[2].wait()


def inputs_kernel(pair_ref, xt_ref):
    height, packed = pair_ref.shape[0] // 2, pair_ref.shape[1]
    x_ref = pair_ref.at[height:]
    pairs = packed // LANES
    rows = pairs * height
    x = jnp.concatenate([x_ref[:, LANES * j : LANES * (j + 1)] for j in range(pairs)], axis=0)
    xt = jnp.transpose(x.astype(jnp.float32))
    h = lax.broadcasted_iota(jnp.int32, (LANES, rows), 1) % height
    xt_ref[0:LANES, :] = jnp.where(h == 0, 0.0, pltpu.roll(xt, 1, 1)).astype(jnp.bfloat16)
    xt_ref[LANES : 2 * LANES, :] = xt.astype(jnp.bfloat16)
    xt_ref[2 * LANES :, :] = jnp.where(h == height - 1, 0.0, pltpu.roll(xt, rows - 1, 1)).astype(jnp.bfloat16)


def weights_kernel(core_ref, w_ref, wt_ref):
    core = core_ref[0]
    zero = jnp.zeros((CH, CH), jnp.bfloat16)
    for slot, od in enumerate((2 - 2 * core, 1, 2 * core)):
        for oh in range(3):
            t = 9 * od + 3 * oh
            before, here, after = w_ref[t], w_ref[t + 1], w_ref[t + 2]
            for parity in range(2):
                if parity == 0:
                    parts = (here, before, zero, after)
                else:
                    parts = (after, here, before, zero)
                r = (2 * oh + parity) * CH
                wt_ref[r : r + CH, 256 * slot : 256 * slot + LANES] = jnp.concatenate(parts[:2], axis=1)
                wt_ref[r : r + CH, 256 * slot + LANES : 256 * (slot + 1)] = jnp.concatenate(parts[2:], axis=1)


def kernel_gradient_kernel(core_ref, far_ref, own_ref, near_ref, xt_own_ref, xt_near_ref, dw_ref, g_ref):
    height, packed = own_ref.shape
    pairs = packed // LANES
    low = lax.broadcasted_iota(jnp.int32, (height, LANES), 1) < CH
    for slot, ref in enumerate((far_ref, own_ref, near_ref)):
        for j in range(pairs):
            at = slice(height * j, height * (j + 1))
            g_ref[at, 256 * slot : 256 * slot + LANES] = ref[0:height, LANES * j : LANES * (j + 1)]
            nothing = jnp.zeros((height, LANES), jnp.bfloat16)
            right = ref[0:height, LANES * (j + 1) : LANES * (j + 2)] if j + 1 < pairs else nothing
            left = ref[0:height, LANES * (j - 1) : LANES * j] if j > 0 else nothing
            g_ref[at, 256 * slot + LANES : 256 * (slot + 1)] = jnp.where(low, right, left)
    d = jnp.dot(xt_own_ref[...], g_ref[:, 0:512], preferred_element_type=jnp.float32)
    d = d + jnp.dot(xt_near_ref[...], g_ref[:, 256:768], preferred_element_type=jnp.float32)
    lo = lax.broadcasted_iota(jnp.int32, (CH, LANES), 1) < CH
    core_0 = jnp.full((CH, LANES), core_ref[0], jnp.int32) == 0

    def block(part, oh, parity, half):
        r = LANES * oh + CH * parity
        c = 256 * part + LANES * half
        return d[r : r + CH, c : c + LANES]

    def swap(v):
        return pltpu.roll(v, CH, 1)

    def two(part, oh):
        return block(part, oh, 0, 0) + jnp.where(lo, swap(block(part, oh, 1, 0)), swap(block(part, oh, 1, 1)))

    def low_one(part, oh):
        return block(part, oh, 1, 0) + swap(block(part, oh, 0, 1))

    def high_one(part, oh):
        return swap(block(part, oh, 1, 0)) + block(part, oh, 0, 1)

    total = jnp.sum(g_ref[:, 256:384].astype(jnp.float32) + g_ref[:, 512:640].astype(jnp.float32), axis=0, keepdims=True)
    first = lax.broadcasted_iota(jnp.int32, (CH, LANES), 0) == 0
    bias = jnp.where(first, jnp.broadcast_to(total + swap(total), (CH, LANES)), 0.0)
    blocks = (
        two(0, 0),
        two(0, 1),
        two(0, 2),
        jnp.where(lo, low_one(0, 0), high_one(0, 1)),
        jnp.where(lo, low_one(0, 2), jnp.where(core_0, high_one(1, 0), high_one(1, 2))),
        jnp.where(core_0, two(1, 0), two(1, 2)),
        jnp.where(core_0, two(1, 1), jnp.where(lo, low_one(1, 1), bias)),
    )
    for i, v in enumerate(blocks):
        dw_ref[CH * i : CH * (i + 1), :] = v


def input_gradient_kernel(g_ref, wt_ref, dx_ref):
    height, packed = dx_ref.shape
    pairs = packed // LANES
    rows = pairs * height
    y = lax.dot_general(
        g_ref[...], wt_ref[...], (((1,), (1,)), ((), ())), preferred_element_type=jnp.float32
    )
    h = lax.broadcasted_iota(jnp.int32, (rows, LANES), 0) % height
    up = jnp.where(h == height - 1, 0.0, pltpu.roll(y[:, :LANES], rows - 1, 0))
    down = jnp.where(h == 0, 0.0, pltpu.roll(y[:, 2 * LANES :], 1, 0))
    out = (y[:, LANES : 2 * LANES] + up + down).astype(jnp.bfloat16)
    for j in range(pairs):
        dx_ref[:, LANES * j : LANES * (j + 1)] = out[height * j : height * (j + 1), :]


def sum_kernel(parts_ref, out_ref):
    group = 4 * CHUNK
    total = parts_ref[0:group, :]
    for i in range(1, parts_ref.shape[0] // group):
        total = total + parts_ref[group * i : group * (i + 1), :]
    s = (total[0:CHUNK] + total[CHUNK : 2 * CHUNK]) + (total[2 * CHUNK : 3 * CHUNK] + total[3 * CHUNK :])
    four = jnp.concatenate([s, s, s, s], axis=0)
    for i in range(out_ref.shape[0] // group):
        out_ref[group * i : group * (i + 1), :] = four


def finish_kernel(parts_ref, out_ref, *, scale):
    s = parts_ref[0:CHUNK, :]
    for i in range(1, parts_ref.shape[0] // CHUNK):
        s = s + parts_ref[CHUNK * i : CHUNK * (i + 1), :]
    s = s * scale
    largest = jnp.max(jnp.abs(s), axis=0, keepdims=True)
    exponent = jnp.floor(jnp.log2(jnp.maximum(largest, 1e-30))) - 14.0
    slot = jnp.concatenate([s * jnp.exp2(-exponent), exponent, jnp.zeros_like(exponent)], axis=0)
    for i in range(out_ref.shape[0] // SLOT):
        out_ref[SLOT * i : SLOT * (i + 1), :] = slot


def unpack_kernel(core_ref, mine_slots_ref, other_slots_ref, weight_ref, bias_ref, mine_ref, other_ref):
    for slots_ref, rows_ref in ((mine_slots_ref, mine_ref), (other_slots_ref, other_ref)):
        for i in range(slots_ref.shape[0] // SLOT):
            unit = jnp.exp2(slots_ref[SLOT * i + CHUNK : SLOT * i + CHUNK + 1, :])
            rows_ref[CHUNK * i : CHUNK * (i + 1), :] = slots_ref[SLOT * i : SLOT * i + CHUNK, :] * unit
    core_0 = jnp.full((CH, LANES), core_ref[0], jnp.int32) == 0
    places = (
        ((19, 18), (22, 21), (25, 24), (20, 23), (26, 11), (10, 9), (13, 12)),
        ((1, 0), (4, 3), (7, 6), (2, 5), (8, 17), (16, 15), (14, None)),
    )
    for half, sides in enumerate(places):
        for i, (lower, upper) in enumerate(sides):
            a = mine_ref[CH * i : CH * (i + 1), :]
            b = other_ref[CH * i : CH * (i + 1), :]
            v = jnp.where(core_0, a, b) if half == 0 else jnp.where(core_0, b, a)
            weight_ref[lower] = v[:, :CH]
            if upper is None:
                bias_ref[...] = v[0:1, CH:]
            else:
                weight_ref[upper] = v[:, CH:]


def in_vmem(array):
    return pltpu.with_memory_space_constraint(array, pltpu.VMEM)


def in_hbm(array):
    return pltpu.with_memory_space_constraint(array, pltpu.HBM)


def sum_and_copy(parts, copies):
    return pl.pallas_call(
        sum_kernel, out_shape=pltpu.VMEM((copies * CHUNK, LANES), jnp.float32), compiler_params=SMALL
    )(in_vmem(parts))


def exchange(rows, axis):
    return lax.all_to_all(rows.reshape(-1, 1, LANES), axis, 0, 0, tiled=True).reshape(-1, LANES)


def on_device(inputs, preact, grad_out, weight):
    chips = lax.axis_size("chip")
    slabs = chips * lax.axis_size("core")
    groups = lax.axis_size("rep")
    _, planes, height, packed = inputs.shape
    count = inputs.shape[0] * groups * planes * slabs * height * (packed // CH)
    scale = 1.0 / float(count) ** 0.5
    core = lax.axis_index("core").astype(jnp.int32).reshape(1)
    in_smem = pl.BlockSpec(memory_space=pltpu.SMEM)
    whole = pl.BlockSpec(memory_space=pltpu.VMEM)
    rows = height * packed // LANES
    own, pack = pl.pallas_call(
        mask_kernel,
        in_specs=[pl.BlockSpec(memory_space=pltpu.HBM)] * 3,
        out_shape=(
            pltpu.VMEM((height, packed), jnp.bfloat16),
            pltpu.VMEM((2 * height, packed), jnp.bfloat16),
        ),
        scratch_shapes=[pltpu.VMEM((height, packed), jnp.bfloat16)] * 2 + [pltpu.SemaphoreType.DMA((3,))],
        compiler_params=SMALL,
        name="mask",
    )(*(in_hbm(a.reshape(height, packed)) for a in (preact, grad_out, inputs)))
    swap = [(0, 1), (1, 0)]
    ends = range(1, slabs - 1, 2)
    far = lax.ppermute(own, ("chip", "core"), [(i, i + 1) for i in ends] + [(i + 1, i) for i in ends])
    near = in_vmem(lax.ppermute(pack, "core", swap))
    wt = pl.pallas_call(
        weights_kernel,
        in_specs=[in_smem, whole],
        out_shape=pltpu.VMEM((3 * LANES, 768), jnp.bfloat16),
        compiler_params=SMALL,
        name="weights",
    )(core, weight.reshape(27, CH, CH))

    def turned(pair):
        return pl.pallas_call(
            inputs_kernel,
            out_shape=pltpu.VMEM((3 * LANES, rows), jnp.bfloat16),
            compiler_params=SMALL,
            name="inputs",
        )(in_vmem(pair))

    dw, g = pl.pallas_call(
        kernel_gradient_kernel,
        in_specs=[in_smem] + [whole] * 5,
        out_shape=(
            pltpu.VMEM((chips * CHUNK, LANES), jnp.float32),
            pltpu.VMEM((rows, 768), jnp.bfloat16),
        ),
        compiler_params=SMALL,
        name="kernel_gradient",
    )(core, in_vmem(far), in_vmem(own), near, in_vmem(turned(pack)), in_vmem(turned(near)))
    dx = pl.pallas_call(
        input_gradient_kernel,
        out_shape=jax.ShapeDtypeStruct((height, packed), jnp.bfloat16),
        compiler_params=SMALL,
        name="input_gradient",
    )(in_vmem(g), in_vmem(wt))
    mine = sum_and_copy(exchange(dw, "chip"), groups)
    total = pl.pallas_call(
        lambda p, o: finish_kernel(p, o, scale=scale),
        out_shape=pltpu.VMEM((chips * SLOT, LANES), jnp.float32),
        compiler_params=SMALL,
        name="finish",
    )(in_vmem(exchange(mine, "rep")))
    gathered = lax.all_to_all(total.astype(jnp.float16), "chip", 0, 0, tiled=True)
    other = lax.ppermute(gathered, "core", swap)
    weight_grad, bias_grad = pl.pallas_call(
        unpack_kernel,
        in_specs=[in_smem, whole, whole],
        out_shape=(
            jax.ShapeDtypeStruct((27, CH, CH), jnp.float32),
            jax.ShapeDtypeStruct((1, CH), jnp.float32),
        ),
        scratch_shapes=[pltpu.VMEM((chips * CHUNK, LANES), jnp.float32)] * 2,
        compiler_params=SMALL,
        name="unpack",
    )(core, in_vmem(gathered.astype(jnp.float32)), in_vmem(other.astype(jnp.float32)))
    return dx.reshape(inputs.shape), weight_grad.reshape(3, 3, 3, CH, CH), bias_grad.reshape(CH)


def solution(mesh):
    groups, slabs = mesh.devices.shape
    by_core = jax.sharding.Mesh(mesh.devices.reshape(groups, slabs // 2, 2), ("rep", "chip", "core"))
    split = P("rep", ("chip", "core"), None, None)
    return jax.shard_map(
        on_device,
        mesh=by_core,
        in_specs=(split, split, split, P()),
        out_specs=(split, P(), P()),
        check_vma=False,
    )
```

```python
import jax
import jax.numpy as jnp
from jax import lax
from jax.experimental import pallas as pl
from jax.experimental.pallas import tpu as pltpu
from jax.sharding import PartitionSpec as P


CH = 64
LANES = 2 * CH
SLOT = 16
CHUNK = 14
SMALL = pltpu.CompilerParams(vmem_limit_bytes=16 * 1024 * 1024)


def mask_kernel(preact_ref, grad_ref, x_ref, own_ref, pack_ref, z_ref, dy_ref, sems):
    height = own_ref.shape[0]
    loads = (
        pltpu.make_async_copy(preact_ref, z_ref, sems.at[0]),
        pltpu.make_async_copy(grad_ref, dy_ref, sems.at[1]),
        pltpu.make_async_copy(x_ref, pack_ref.at[height:], sems.at[2]),
    )
    for load in loads:
        load.start()
    loads[0].wait()
    loads[1].wait()
    own = jnp.where(z_ref[...] > 0, dy_ref[...], jnp.zeros_like(dy_ref))
    own_ref[...] = own
    pack_ref[0:height, :] = own
    loads[2].wait()


def inputs_kernel(pair_ref, xt_ref):
    height, packed = pair_ref.shape[0] // 2, pair_ref.shape[1]
    x_ref = pair_ref.at[height:]
    pairs = packed // LANES
    rows = pairs * height
    x = jnp.concatenate([x_ref[:, LANES * j : LANES * (j + 1)] for j in range(pairs)], axis=0)
    xt = jnp.transpose(x.astype(jnp.float32))
    h = lax.broadcasted_iota(jnp.int32, (LANES, rows), 1) % height
    xt_ref[0:LANES, :] = jnp.where(h == 0, 0.0, pltpu.roll(xt, 1, 1)).astype(jnp.bfloat16)
    xt_ref[LANES : 2 * LANES, :] = xt.astype(jnp.bfloat16)
    xt_ref[2 * LANES :, :] = jnp.where(h == height - 1, 0.0, pltpu.roll(xt, rows - 1, 1)).astype(jnp.bfloat16)


def weights_kernel(core_ref, w_ref, wt_ref):
    core = core_ref[0]
    zero = jnp.zeros((CH, CH), jnp.bfloat16)
    for slot, od in enumerate((2 - 2 * core, 1, 2 * core)):
        for oh in range(3):
            t = 9 * od + 3 * oh
            before, here, after = w_ref[t], w_ref[t + 1], w_ref[t + 2]
            for parity in range(2):
                if parity == 0:
                    parts = (here, before, zero, after)
                else:
                    parts = (after, here, before, zero)
                r = (2 * oh + parity) * CH
                wt_ref[r : r + CH, 256 * slot : 256 * slot + LANES] = jnp.concatenate(parts[:2], axis=1)
                wt_ref[r : r + CH, 256 * slot + LANES : 256 * (slot + 1)] = jnp.concatenate(parts[2:], axis=1)


def kernel_gradient_kernel(core_ref, far_ref, own_ref, near_ref, xt_own_ref, xt_near_ref, dw_ref, g_ref):
    height, packed = own_ref.shape
    pairs = packed // LANES
    low = lax.broadcasted_iota(jnp.int32, (height, LANES), 1) < CH
    for slot, ref in enumerate((far_ref, own_ref, near_ref)):
        for j in range(pairs):
            at = slice(height * j, height * (j + 1))
            g_ref[at, 256 * slot : 256 * slot + LANES] = ref[0:height, LANES * j : LANES * (j + 1)]
            nothing = jnp.zeros((height, LANES), jnp.bfloat16)
            right = ref[0:height, LANES * (j + 1) : LANES * (j + 2)] if j + 1 < pairs else nothing
            left = ref[0:height, LANES * (j - 1) : LANES * j] if j > 0 else nothing
            g_ref[at, 256 * slot + LANES : 256 * (slot + 1)] = jnp.where(low, right, left)
    d = jnp.dot(xt_own_ref[...], g_ref[:, 0:512], preferred_element_type=jnp.float32)
    d = d + jnp.dot(xt_near_ref[...], g_ref[:, 256:768], preferred_element_type=jnp.float32)
    lo = lax.broadcasted_iota(jnp.int32, (CH, LANES), 1) < CH
    core_0 = jnp.full((CH, LANES), core_ref[0], jnp.int32) == 0

    def block(part, oh, parity, half):
        r = LANES * oh + CH * parity
        c = 256 * part + LANES * half
        return d[r : r + CH, c : c + LANES]

    def swap(v):
        return pltpu.roll(v, CH, 1)

    def two(part, oh):
        return block(part, oh, 0, 0) + jnp.where(lo, swap(block(part, oh, 1, 0)), swap(block(part, oh, 1, 1)))

    def low_one(part, oh):
        return block(part, oh, 1, 0) + swap(block(part, oh, 0, 1))

    def high_one(part, oh):
        return swap(block(part, oh, 1, 0)) + block(part, oh, 0, 1)

    total = jnp.sum(g_ref[:, 256:384].astype(jnp.float32) + g_ref[:, 512:640].astype(jnp.float32), axis=0, keepdims=True)
    first = lax.broadcasted_iota(jnp.int32, (CH, LANES), 0) == 0
    bias = jnp.where(first, jnp.broadcast_to(total + swap(total), (CH, LANES)), 0.0)
    blocks = (
        two(0, 0),
        two(0, 1),
        two(0, 2),
        jnp.where(lo, low_one(0, 0), high_one(0, 1)),
        jnp.where(lo, low_one(0, 2), jnp.where(core_0, high_one(1, 0), high_one(1, 2))),
        jnp.where(core_0, two(1, 0), two(1, 2)),
        jnp.where(core_0, two(1, 1), jnp.where(lo, low_one(1, 1), bias)),
    )
    for i, v in enumerate(blocks):
        dw_ref[CH * i : CH * (i + 1), :] = v


def input_gradient_kernel(g_ref, wt_ref, dx_ref):
    height, packed = dx_ref.shape
    pairs = packed // LANES
    rows = pairs * height
    y = lax.dot_general(
        g_ref[...], wt_ref[...], (((1,), (1,)), ((), ())), preferred_element_type=jnp.float32
    )
    h = lax.broadcasted_iota(jnp.int32, (rows, LANES), 0) % height
    up = jnp.where(h == height - 1, 0.0, pltpu.roll(y[:, :LANES], rows - 1, 0))
    down = jnp.where(h == 0, 0.0, pltpu.roll(y[:, 2 * LANES :], 1, 0))
    out = (y[:, LANES : 2 * LANES] + up + down).astype(jnp.bfloat16)
    for j in range(pairs):
        dx_ref[:, LANES * j : LANES * (j + 1)] = out[height * j : height * (j + 1), :]


def to_slot(rows):
    largest = jnp.max(jnp.abs(rows), axis=0, keepdims=True)
    exponent = jnp.floor(jnp.log2(jnp.maximum(largest, 1e-30))) - 14.0
    rest = [exponent, jnp.zeros((SLOT - CHUNK - 1, LANES), jnp.float32)]
    return jnp.concatenate([rows * jnp.exp2(-exponent)] + rest, axis=0)


def from_slot(slots_ref, i):
    unit = jnp.exp2(slots_ref[SLOT * i + CHUNK : SLOT * i + CHUNK + 1, :])
    return slots_ref[SLOT * i : SLOT * i + CHUNK, :] * unit


def plane_sum_kernel(parts_ref, out_ref):
    group = 4 * CHUNK
    total = parts_ref[0:group, :]
    for i in range(1, parts_ref.shape[0] // group):
        total = total + parts_ref[group * i : group * (i + 1), :]
    s = (total[0:CHUNK] + total[CHUNK : 2 * CHUNK]) + (total[2 * CHUNK : 3 * CHUNK] + total[3 * CHUNK :])
    slot = to_slot(s)
    for i in range(out_ref.shape[0] // SLOT):
        out_ref[SLOT * i : SLOT * (i + 1), :] = slot


def finish_kernel(slots_ref, out_ref, *, scale):
    for core in range(2):
        s = from_slot(slots_ref, core)
        for i in range(core + 2, slots_ref.shape[0] // SLOT, 2):
            s = s + from_slot(slots_ref, i)
        slot = to_slot(s * scale)
        for i in range(core, out_ref.shape[0] // SLOT, 2):
            out_ref[SLOT * i : SLOT * (i + 1), :] = slot


def unpack_kernel(slots_ref, weight_ref, bias_ref, rows_ref):
    chips = slots_ref.shape[0] // (2 * SLOT)
    places = (
        ((19, 18), (22, 21), (25, 24), (20, 23), (26, 11), (10, 9), (13, 12)),
        ((1, 0), (4, 3), (7, 6), (2, 5), (8, 17), (16, 15), (14, None)),
    )
    for core, sides in enumerate(places):
        for i in range(chips):
            rows_ref[CHUNK * i : CHUNK * (i + 1), :] = from_slot(slots_ref, 2 * i + core)
        for i, (lower, upper) in enumerate(sides):
            v = rows_ref[CH * i : CH * (i + 1), :]
            weight_ref[lower] = v[:, :CH]
            if upper is None:
                bias_ref[...] = v[0:1, CH:]
            else:
                weight_ref[upper] = v[:, CH:]


def in_vmem(array):
    return pltpu.with_memory_space_constraint(array, pltpu.VMEM)


def in_hbm(array):
    return pltpu.with_memory_space_constraint(array, pltpu.HBM)


def exchange(slots, axis):
    half = slots.astype(jnp.float16)
    return in_vmem(lax.all_to_all(half, axis, 0, 0, tiled=True).astype(jnp.float32))


def on_device(inputs, preact, grad_out, weight):
    chips = lax.axis_size("chip")
    slabs = chips * lax.axis_size("core")
    groups = lax.axis_size("rep")
    _, planes, height, packed = inputs.shape
    count = inputs.shape[0] * groups * planes * slabs * height * (packed // CH)
    scale = 1.0 / float(count) ** 0.5
    core = lax.axis_index("core").astype(jnp.int32).reshape(1)
    in_smem = pl.BlockSpec(memory_space=pltpu.SMEM)
    whole = pl.BlockSpec(memory_space=pltpu.VMEM)
    rows = height * packed // LANES
    own, pack = pl.pallas_call(
        mask_kernel,
        in_specs=[pl.BlockSpec(memory_space=pltpu.HBM)] * 3,
        out_shape=(
            pltpu.VMEM((height, packed), jnp.bfloat16),
            pltpu.VMEM((2 * height, packed), jnp.bfloat16),
        ),
        scratch_shapes=[pltpu.VMEM((height, packed), jnp.bfloat16)] * 2 + [pltpu.SemaphoreType.DMA((3,))],
        compiler_params=SMALL,
        name="mask",
    )(*(in_hbm(a.reshape(height, packed)) for a in (preact, grad_out, inputs)))
    swap = [(0, 1), (1, 0)]
    ends = range(1, slabs - 1, 2)
    far = lax.ppermute(own, ("chip", "core"), [(i, i + 1) for i in ends] + [(i + 1, i) for i in ends])
    near = in_vmem(lax.ppermute(pack, "core", swap))
    wt = pl.pallas_call(
        weights_kernel,
        in_specs=[in_smem, whole],
        out_shape=pltpu.VMEM((3 * LANES, 768), jnp.bfloat16),
        compiler_params=SMALL,
        name="weights",
    )(core, weight.reshape(27, CH, CH))

    def turned(pair):
        return pl.pallas_call(
            inputs_kernel,
            out_shape=pltpu.VMEM((3 * LANES, rows), jnp.bfloat16),
            compiler_params=SMALL,
            name="inputs",
        )(in_vmem(pair))

    dw, g = pl.pallas_call(
        kernel_gradient_kernel,
        in_specs=[in_smem] + [whole] * 5,
        out_shape=(
            pltpu.VMEM((chips * CHUNK, LANES), jnp.float32),
            pltpu.VMEM((rows, 768), jnp.bfloat16),
        ),
        compiler_params=SMALL,
        name="kernel_gradient",
    )(core, in_vmem(far), in_vmem(own), near, in_vmem(turned(pack)), in_vmem(turned(near)))
    dx = pl.pallas_call(
        input_gradient_kernel,
        out_shape=jax.ShapeDtypeStruct((height, packed), jnp.bfloat16),
        compiler_params=SMALL,
        name="input_gradient",
    )(in_vmem(g), in_vmem(wt))
    parts = lax.all_to_all(dw.reshape(-1, 1, LANES), "chip", 0, 0, tiled=True).reshape(-1, LANES)
    mine = pl.pallas_call(
        plane_sum_kernel,
        out_shape=pltpu.VMEM((groups * 2 * SLOT, LANES), jnp.float32),
        compiler_params=SMALL,
        name="plane_sum",
    )(in_vmem(parts))
    total = pl.pallas_call(
        lambda p, o: finish_kernel(p, o, scale=scale),
        out_shape=pltpu.VMEM((chips * 2 * SLOT, LANES), jnp.float32),
        compiler_params=SMALL,
        name="finish",
    )(exchange(mine, ("rep", "core")))
    weight_grad, bias_grad = pl.pallas_call(
        unpack_kernel,
        out_shape=(
            jax.ShapeDtypeStruct((27, CH, CH), jnp.float32),
            jax.ShapeDtypeStruct((1, CH), jnp.float32),
        ),
        scratch_shapes=[pltpu.VMEM((chips * CHUNK, LANES), jnp.float32)],
        compiler_params=SMALL,
        name="unpack",
    )(exchange(total, "chip"))
    return dx.reshape(inputs.shape), weight_grad.reshape(3, 3, 3, CH, CH), bias_grad.reshape(CH)


def solution(mesh):
    groups, slabs = mesh.devices.shape
    by_core = jax.sharding.Mesh(mesh.devices.reshape(groups, slabs // 2, 2), ("rep", "chip", "core"))
    split = P("rep", ("chip", "core"), None, None)
    return jax.shard_map(
        on_device,
        mesh=by_core,
        in_specs=(split, split, split, P()),
        out_specs=(split, P(), P()),
        check_vma=False,
    )
```

```python
import jax
import jax.numpy as jnp
from jax import lax
from jax.experimental import pallas as pl
from jax.experimental.pallas import tpu as pltpu
from jax.sharding import PartitionSpec as P


CH = 64
LANES = 2 * CH
SLOT = 16
CHUNK = 14
SMALL = pltpu.CompilerParams(vmem_limit_bytes=16 * 1024 * 1024)


def mask_kernel(preact_ref, grad_ref, x_ref, own_ref, pack_ref, z_ref, dy_ref, sems):
    height = own_ref.shape[0]
    loads = (
        pltpu.make_async_copy(preact_ref, z_ref, sems.at[0]),
        pltpu.make_async_copy(grad_ref, dy_ref, sems.at[1]),
        pltpu.make_async_copy(x_ref, pack_ref.at[height:], sems.at[2]),
    )
    for load in loads:
        load.start()
    loads[0].wait()
    loads[1].wait()
    own = jnp.where(z_ref[...] > 0, dy_ref[...], jnp.zeros_like(dy_ref))
    own_ref[...] = own
    pack_ref[0:height, :] = own
    loads[2].wait()


def inputs_kernel(pair_ref, xt_ref):
    height, packed = pair_ref.shape[0] // 2, pair_ref.shape[1]
    x_ref = pair_ref.at[height:]
    pairs = packed // LANES
    rows = pairs * height
    x = jnp.concatenate([x_ref[:, LANES * j : LANES * (j + 1)] for j in range(pairs)], axis=0)
    xt = jnp.transpose(x.astype(jnp.float32))
    h = lax.broadcasted_iota(jnp.int32, (LANES, rows), 1) % height
    xt_ref[0:LANES, :] = jnp.where(h == 0, 0.0, pltpu.roll(xt, 1, 1)).astype(jnp.bfloat16)
    xt_ref[LANES : 2 * LANES, :] = xt.astype(jnp.bfloat16)
    xt_ref[2 * LANES :, :] = jnp.where(h == height - 1, 0.0, pltpu.roll(xt, rows - 1, 1)).astype(jnp.bfloat16)


def weights_kernel(core_ref, w_ref, wt_ref):
    core = core_ref[0]
    zero = jnp.zeros((CH, CH), jnp.bfloat16)
    for slot, od in enumerate((2 - 2 * core, 1, 2 * core)):
        for oh in range(3):
            t = 9 * od + 3 * oh
            before, here, after = w_ref[t], w_ref[t + 1], w_ref[t + 2]
            for parity in range(2):
                if parity == 0:
                    parts = (here, before, zero, after)
                else:
                    parts = (after, here, before, zero)
                r = (2 * oh + parity) * CH
                wt_ref[r : r + CH, 256 * slot : 256 * slot + LANES] = jnp.concatenate(parts[:2], axis=1)
                wt_ref[r : r + CH, 256 * slot + LANES : 256 * (slot + 1)] = jnp.concatenate(parts[2:], axis=1)


def kernel_gradient_kernel(core_ref, far_ref, own_ref, near_ref, xt_own_ref, xt_near_ref, slots_ref, g_ref, dw_ref):
    height, packed = own_ref.shape
    pairs = packed // LANES
    low = lax.broadcasted_iota(jnp.int32, (height, LANES), 1) < CH
    for slot, ref in enumerate((far_ref, own_ref, near_ref)):
        for j in range(pairs):
            at = slice(height * j, height * (j + 1))
            g_ref[at, 256 * slot : 256 * slot + LANES] = ref[0:height, LANES * j : LANES * (j + 1)]
            nothing = jnp.zeros((height, LANES), jnp.bfloat16)
            right = ref[0:height, LANES * (j + 1) : LANES * (j + 2)] if j + 1 < pairs else nothing
            left = ref[0:height, LANES * (j - 1) : LANES * j] if j > 0 else nothing
            g_ref[at, 256 * slot + LANES : 256 * (slot + 1)] = jnp.where(low, right, left)
    d = jnp.dot(xt_own_ref[...], g_ref[:, 0:512], preferred_element_type=jnp.float32)
    d = d + jnp.dot(xt_near_ref[...], g_ref[:, 256:768], preferred_element_type=jnp.float32)
    lo = lax.broadcasted_iota(jnp.int32, (CH, LANES), 1) < CH
    core_0 = jnp.full((CH, LANES), core_ref[0], jnp.int32) == 0

    def block(part, oh, parity, half):
        r = LANES * oh + CH * parity
        c = 256 * part + LANES * half
        return d[r : r + CH, c : c + LANES]

    def swap(v):
        return pltpu.roll(v, CH, 1)

    def two(part, oh):
        return block(part, oh, 0, 0) + jnp.where(lo, swap(block(part, oh, 1, 0)), swap(block(part, oh, 1, 1)))

    def low_one(part, oh):
        return block(part, oh, 1, 0) + swap(block(part, oh, 0, 1))

    def high_one(part, oh):
        return swap(block(part, oh, 1, 0)) + block(part, oh, 0, 1)

    total = jnp.sum(g_ref[:, 256:384].astype(jnp.float32) + g_ref[:, 512:640].astype(jnp.float32), axis=0, keepdims=True)
    first = lax.broadcasted_iota(jnp.int32, (CH, LANES), 0) == 0
    bias = jnp.where(first, jnp.broadcast_to(total + swap(total), (CH, LANES)), 0.0)
    blocks = (
        two(0, 0),
        two(0, 1),
        two(0, 2),
        jnp.where(lo, low_one(0, 0), high_one(0, 1)),
        jnp.where(lo, low_one(0, 2), jnp.where(core_0, high_one(1, 0), high_one(1, 2))),
        jnp.where(core_0, two(1, 0), two(1, 2)),
        jnp.where(core_0, two(1, 1), jnp.where(lo, low_one(1, 1), bias)),
    )
    largest = jnp.max(jnp.abs(blocks[0]), axis=0, keepdims=True)
    for v in blocks[1:]:
        largest = jnp.maximum(largest, jnp.max(jnp.abs(v), axis=0, keepdims=True))
    exponent = exponents(largest)
    unit = jnp.exp2(-exponent)
    for i, v in enumerate(blocks):
        dw_ref[CH * i : CH * (i + 1), :] = v * unit
    for i in range(slots_ref.shape[0] // SLOT):
        slots_ref[SLOT * i : SLOT * (i + 1), :] = to_slot(dw_ref[CHUNK * i : CHUNK * (i + 1), :], exponent)


def input_gradient_kernel(g_ref, wt_ref, dx_ref):
    height, packed = dx_ref.shape
    pairs = packed // LANES
    rows = pairs * height
    y = lax.dot_general(
        g_ref[...], wt_ref[...], (((1,), (1,)), ((), ())), preferred_element_type=jnp.float32
    )
    h = lax.broadcasted_iota(jnp.int32, (rows, LANES), 0) % height
    up = jnp.where(h == height - 1, 0.0, pltpu.roll(y[:, :LANES], rows - 1, 0))
    down = jnp.where(h == 0, 0.0, pltpu.roll(y[:, 2 * LANES :], 1, 0))
    out = (y[:, LANES : 2 * LANES] + up + down).astype(jnp.bfloat16)
    for j in range(pairs):
        dx_ref[:, LANES * j : LANES * (j + 1)] = out[height * j : height * (j + 1), :]


def exponents(largest):
    return jnp.floor(jnp.log2(jnp.maximum(largest, 1e-30))) - 14.0


def to_slot(rows, exponent):
    return jnp.concatenate([rows, exponent, jnp.zeros((SLOT - CHUNK - 1, LANES), jnp.float32)], axis=0)


def from_slot(slots_ref, i):
    unit = jnp.exp2(slots_ref[SLOT * i + CHUNK : SLOT * i + CHUNK + 1, :])
    return slots_ref[SLOT * i : SLOT * i + CHUNK, :] * unit


def plane_sum_kernel(slots_ref, out_ref):
    sums = [from_slot(slots_ref, i) for i in range(slots_ref.shape[0] // SLOT)]
    while len(sums) > 1:
        sums = [a + b for a, b in zip(sums[::2], sums[1::2], strict=True)]
    for i in range(out_ref.shape[0] // CHUNK):
        out_ref[CHUNK * i : CHUNK * (i + 1), :] = sums[0]


def finish_kernel(parts_ref, out_ref, *, scale):
    s = parts_ref[0:CHUNK, :]
    for i in range(1, parts_ref.shape[0] // CHUNK):
        s = s + parts_ref[CHUNK * i : CHUNK * (i + 1), :]
    s = s * scale
    exponent = exponents(jnp.max(jnp.abs(s), axis=0, keepdims=True))
    slot = to_slot(s * jnp.exp2(-exponent), exponent)
    for i in range(out_ref.shape[0] // SLOT):
        out_ref[SLOT * i : SLOT * (i + 1), :] = slot


def unpack_kernel(core_ref, mine_slots_ref, other_slots_ref, weight_ref, bias_ref, mine_ref, other_ref):
    for slots_ref, rows_ref in ((mine_slots_ref, mine_ref), (other_slots_ref, other_ref)):
        for i in range(slots_ref.shape[0] // SLOT):
            rows_ref[CHUNK * i : CHUNK * (i + 1), :] = from_slot(slots_ref, i)
    core_0 = jnp.full((CH, LANES), core_ref[0], jnp.int32) == 0
    places = (
        ((19, 18), (22, 21), (25, 24), (20, 23), (26, 11), (10, 9), (13, 12)),
        ((1, 0), (4, 3), (7, 6), (2, 5), (8, 17), (16, 15), (14, None)),
    )
    for half, sides in enumerate(places):
        for i, (lower, upper) in enumerate(sides):
            a = mine_ref[CH * i : CH * (i + 1), :]
            b = other_ref[CH * i : CH * (i + 1), :]
            v = jnp.where(core_0, a, b) if half == 0 else jnp.where(core_0, b, a)
            weight_ref[lower] = v[:, :CH]
            if upper is None:
                bias_ref[...] = v[0:1, CH:]
            else:
                weight_ref[upper] = v[:, CH:]


def in_vmem(array):
    return pltpu.with_memory_space_constraint(array, pltpu.VMEM)


def in_hbm(array):
    return pltpu.with_memory_space_constraint(array, pltpu.HBM)


def exchange(rows, axis):
    return in_vmem(lax.all_to_all(rows.reshape(-1, 1, LANES), axis, 0, 0, tiled=True).reshape(-1, LANES))


def exchange_slots(slots):
    return lax.all_to_all(slots.astype(jnp.float16), "chip", 0, 0, tiled=True)


def on_device(inputs, preact, grad_out, weight):
    chips = lax.axis_size("chip")
    slabs = chips * lax.axis_size("core")
    groups = lax.axis_size("rep")
    _, planes, height, packed = inputs.shape
    count = inputs.shape[0] * groups * planes * slabs * height * (packed // CH)
    scale = 1.0 / float(count) ** 0.5
    core = lax.axis_index("core").astype(jnp.int32).reshape(1)
    in_smem = pl.BlockSpec(memory_space=pltpu.SMEM)
    whole = pl.BlockSpec(memory_space=pltpu.VMEM)
    rows = height * packed // LANES
    own, pack = pl.pallas_call(
        mask_kernel,
        in_specs=[pl.BlockSpec(memory_space=pltpu.HBM)] * 3,
        out_shape=(
            pltpu.VMEM((height, packed), jnp.bfloat16),
            pltpu.VMEM((2 * height, packed), jnp.bfloat16),
        ),
        scratch_shapes=[pltpu.VMEM((height, packed), jnp.bfloat16)] * 2 + [pltpu.SemaphoreType.DMA((3,))],
        compiler_params=SMALL,
        name="mask",
    )(*(in_hbm(a.reshape(height, packed)) for a in (preact, grad_out, inputs)))
    swap = [(0, 1), (1, 0)]
    ends = range(1, slabs - 1, 2)
    far = lax.ppermute(own, ("chip", "core"), [(i, i + 1) for i in ends] + [(i + 1, i) for i in ends])
    near = in_vmem(lax.ppermute(pack, "core", swap))
    wt = pl.pallas_call(
        weights_kernel,
        in_specs=[in_smem, whole],
        out_shape=pltpu.VMEM((3 * LANES, 768), jnp.bfloat16),
        compiler_params=SMALL,
        name="weights",
    )(core, weight.reshape(27, CH, CH))

    def turned(pair):
        return pl.pallas_call(
            inputs_kernel,
            out_shape=pltpu.VMEM((3 * LANES, rows), jnp.bfloat16),
            compiler_params=SMALL,
            name="inputs",
        )(in_vmem(pair))

    dw, g = pl.pallas_call(
        kernel_gradient_kernel,
        in_specs=[in_smem] + [whole] * 5,
        out_shape=(
            pltpu.VMEM((chips * SLOT, LANES), jnp.float32),
            pltpu.VMEM((rows, 768), jnp.bfloat16),
        ),
        scratch_shapes=[pltpu.VMEM((chips * CHUNK, LANES), jnp.float32)],
        compiler_params=SMALL,
        name="kernel_gradient",
    )(core, in_vmem(far), in_vmem(own), near, in_vmem(turned(pack)), in_vmem(turned(near)))
    mine = pl.pallas_call(
        plane_sum_kernel,
        out_shape=pltpu.VMEM((groups * CHUNK, LANES), jnp.float32),
        compiler_params=SMALL,
        name="plane_sum",
    )(in_vmem(exchange_slots(dw).astype(jnp.float32)))
    total = pl.pallas_call(
        lambda p, o: finish_kernel(p, o, scale=scale),
        out_shape=pltpu.VMEM((chips * SLOT, LANES), jnp.float32),
        compiler_params=SMALL,
        name="finish",
    )(exchange(mine, "rep"))
    gathered = exchange_slots(total)
    other = lax.ppermute(gathered, "core", swap)
    dx = pl.pallas_call(
        input_gradient_kernel,
        out_shape=jax.ShapeDtypeStruct((height, packed), jnp.bfloat16),
        compiler_params=SMALL,
        name="input_gradient",
    )(in_vmem(g), in_vmem(wt))
    weight_grad, bias_grad = pl.pallas_call(
        unpack_kernel,
        in_specs=[in_smem, whole, whole],
        out_shape=(
            jax.ShapeDtypeStruct((27, CH, CH), jnp.float32),
            jax.ShapeDtypeStruct((1, CH), jnp.float32),
        ),
        scratch_shapes=[pltpu.VMEM((chips * CHUNK, LANES), jnp.float32)] * 2,
        compiler_params=SMALL,
        name="unpack",
    )(core, in_vmem(gathered.astype(jnp.float32)), in_vmem(other.astype(jnp.float32)))
    return dx.reshape(inputs.shape), weight_grad.reshape(3, 3, 3, CH, CH), bias_grad.reshape(CH)


def solution(mesh):
    groups, slabs = mesh.devices.shape
    by_core = jax.sharding.Mesh(mesh.devices.reshape(groups, slabs // 2, 2), ("rep", "chip", "core"))
    split = P("rep", ("chip", "core"), None, None)
    return jax.shard_map(
        on_device,
        mesh=by_core,
        in_specs=(split, split, split, P()),
        out_specs=(split, P(), P()),
        check_vma=False,
    )
```

```python
import jax
import jax.numpy as jnp
from jax import lax
from jax.experimental import pallas as pl
from jax.experimental.pallas import tpu as pltpu
from jax.sharding import PartitionSpec as P


CH = 64
LANES = 2 * CH
SLOT = 16
CHUNK = 14
SMALL = pltpu.CompilerParams(vmem_limit_bytes=16 * 1024 * 1024)


def mask_kernel(preact_ref, grad_ref, x_ref, own_ref, pack_ref, z_ref, dy_ref, sems):
    height = own_ref.shape[0]
    loads = (
        pltpu.make_async_copy(preact_ref, z_ref, sems.at[0]),
        pltpu.make_async_copy(grad_ref, dy_ref, sems.at[1]),
        pltpu.make_async_copy(x_ref, pack_ref.at[height:], sems.at[2]),
    )
    for load in loads:
        load.start()
    loads[0].wait()
    loads[1].wait()
    own = jnp.where(z_ref[...] > 0, dy_ref[...], jnp.zeros_like(dy_ref))
    own_ref[...] = own
    pack_ref[0:height, :] = own
    loads[2].wait()


def inputs_kernel(pair_ref, xt_ref):
    height, packed = pair_ref.shape[0] // 2, pair_ref.shape[1]
    x_ref = pair_ref.at[height:]
    pairs = packed // LANES
    rows = pairs * height
    x = jnp.concatenate([x_ref[:, LANES * j : LANES * (j + 1)] for j in range(pairs)], axis=0)
    xt = jnp.transpose(x.astype(jnp.float32))
    h = lax.broadcasted_iota(jnp.int32, (LANES, rows), 1) % height
    xt_ref[0:LANES, :] = jnp.where(h == 0, 0.0, pltpu.roll(xt, 1, 1)).astype(jnp.bfloat16)
    xt_ref[LANES : 2 * LANES, :] = xt.astype(jnp.bfloat16)
    xt_ref[2 * LANES :, :] = jnp.where(h == height - 1, 0.0, pltpu.roll(xt, rows - 1, 1)).astype(jnp.bfloat16)


def weights_kernel(core_ref, w_ref, wt_ref):
    core = core_ref[0]
    zero = jnp.zeros((CH, CH), jnp.bfloat16)
    for slot, od in enumerate((2 - 2 * core, 1, 2 * core)):
        for oh in range(3):
            t = 9 * od + 3 * oh
            before, here, after = w_ref[t], w_ref[t + 1], w_ref[t + 2]
            for parity in range(2):
                if parity == 0:
                    parts = (here, before, zero, after)
                else:
                    parts = (after, here, before, zero)
                r = (2 * oh + parity) * CH
                wt_ref[r : r + CH, 256 * slot : 256 * slot + LANES] = jnp.concatenate(parts[:2], axis=1)
                wt_ref[r : r + CH, 256 * slot + LANES : 256 * (slot + 1)] = jnp.concatenate(parts[2:], axis=1)


def kernel_gradient_kernel(core_ref, far_ref, own_ref, near_ref, xt_own_ref, xt_near_ref, slots_ref, g_ref, dw_ref):
    height, packed = own_ref.shape
    pairs = packed // LANES
    low = lax.broadcasted_iota(jnp.int32, (height, LANES), 1) < CH
    for slot, ref in enumerate((far_ref, own_ref, near_ref)):
        for j in range(pairs):
            at = slice(height * j, height * (j + 1))
            g_ref[at, 256 * slot : 256 * slot + LANES] = ref[0:height, LANES * j : LANES * (j + 1)]
            nothing = jnp.zeros((height, LANES), jnp.bfloat16)
            right = ref[0:height, LANES * (j + 1) : LANES * (j + 2)] if j + 1 < pairs else nothing
            left = ref[0:height, LANES * (j - 1) : LANES * j] if j > 0 else nothing
            g_ref[at, 256 * slot + LANES : 256 * (slot + 1)] = jnp.where(low, right, left)
    d = jnp.dot(xt_own_ref[...], g_ref[:, 0:512], preferred_element_type=jnp.float32)
    d = d + jnp.dot(xt_near_ref[...], g_ref[:, 256:768], preferred_element_type=jnp.float32)
    lo = lax.broadcasted_iota(jnp.int32, (CH, LANES), 1) < CH
    core_0 = jnp.full((CH, LANES), core_ref[0], jnp.int32) == 0

    def block(part, oh, parity, half):
        r = LANES * oh + CH * parity
        c = 256 * part + LANES * half
        return d[r : r + CH, c : c + LANES]

    def swap(v):
        return pltpu.roll(v, CH, 1)

    def two(part, oh):
        return block(part, oh, 0, 0) + jnp.where(lo, swap(block(part, oh, 1, 0)), swap(block(part, oh, 1, 1)))

    def low_one(part, oh):
        return block(part, oh, 1, 0) + swap(block(part, oh, 0, 1))

    def high_one(part, oh):
        return swap(block(part, oh, 1, 0)) + block(part, oh, 0, 1)

    total = jnp.sum(g_ref[:, 256:384].astype(jnp.float32) + g_ref[:, 512:640].astype(jnp.float32), axis=0, keepdims=True)
    first = lax.broadcasted_iota(jnp.int32, (CH, LANES), 0) == 0
    bias = jnp.where(first, jnp.broadcast_to(total + swap(total), (CH, LANES)), 0.0)
    blocks = (
        two(0, 0),
        two(0, 1),
        two(0, 2),
        jnp.where(lo, low_one(0, 0), high_one(0, 1)),
        jnp.where(lo, low_one(0, 2), jnp.where(core_0, high_one(1, 0), high_one(1, 2))),
        jnp.where(core_0, two(1, 0), two(1, 2)),
        jnp.where(core_0, two(1, 1), jnp.where(lo, low_one(1, 1), bias)),
    )
    largest = jnp.max(jnp.abs(blocks[0]), axis=0, keepdims=True)
    for v in blocks[1:]:
        largest = jnp.maximum(largest, jnp.max(jnp.abs(v), axis=0, keepdims=True))
    exponent = exponents(largest)
    unit = jnp.exp2(-exponent)
    for i, v in enumerate(blocks):
        dw_ref[CH * i : CH * (i + 1), :] = v * unit
    for i in range(slots_ref.shape[0] // SLOT):
        slots_ref[SLOT * i : SLOT * (i + 1), :] = to_slot(dw_ref[CHUNK * i : CHUNK * (i + 1), :], exponent)


def input_gradient_kernel(g_ref, wt_ref, dx_ref):
    height, packed = dx_ref.shape
    pairs = packed // LANES
    rows = pairs * height
    y = lax.dot_general(
        g_ref[...], wt_ref[...], (((1,), (1,)), ((), ())), preferred_element_type=jnp.float32
    )
    h = lax.broadcasted_iota(jnp.int32, (rows, LANES), 0) % height
    up = jnp.where(h == height - 1, 0.0, pltpu.roll(y[:, :LANES], rows - 1, 0))
    down = jnp.where(h == 0, 0.0, pltpu.roll(y[:, 2 * LANES :], 1, 0))
    out = (y[:, LANES : 2 * LANES] + up + down).astype(jnp.bfloat16)
    for j in range(pairs):
        dx_ref[:, LANES * j : LANES * (j + 1)] = out[height * j : height * (j + 1), :]


def exponents(largest):
    return jnp.floor(jnp.log2(jnp.maximum(largest, 1e-30))) - 14.0


def to_slot(rows, exponent):
    return jnp.concatenate([rows, exponent, jnp.zeros((SLOT - CHUNK - 1, LANES), jnp.float32)], axis=0)


def from_slot(slots_ref, i):
    unit = jnp.exp2(slots_ref[SLOT * i + CHUNK : SLOT * i + CHUNK + 1, :])
    return slots_ref[SLOT * i : SLOT * i + CHUNK, :] * unit


def plane_sum_kernel(slots_ref, out_ref):
    sums = [from_slot(slots_ref, i) for i in range(slots_ref.shape[0] // SLOT)]
    while len(sums) > 1:
        sums = [a + b for a, b in zip(sums[::2], sums[1::2], strict=True)]
    for i in range(out_ref.shape[0] // CHUNK):
        out_ref[CHUNK * i : CHUNK * (i + 1), :] = sums[0]


def finish_kernel(parts_ref, out_ref, *, scale):
    s = parts_ref[0:CHUNK, :]
    for i in range(1, parts_ref.shape[0] // CHUNK):
        s = s + parts_ref[CHUNK * i : CHUNK * (i + 1), :]
    s = s * scale
    exponent = exponents(jnp.max(jnp.abs(s), axis=0, keepdims=True))
    slot = to_slot(s * jnp.exp2(-exponent), exponent)
    for i in range(out_ref.shape[0] // SLOT):
        out_ref[SLOT * i : SLOT * (i + 1), :] = slot


def unpack_kernel(
    core_ref, mine_ref, other_ref, dx_ref, weight_ref, bias_ref, dx_out_ref, rows_ref, taps_ref, last_ref, sems
):
    stores = [pltpu.make_async_copy(dx_ref, dx_out_ref, sems.at[0])]
    stores[0].start()
    chips = mine_ref.shape[0] // SLOT
    places = (
        (((19, 18), (22, 21), (25, 24), (20, 23), (26, 11), (10, 9), (13, 12)), ((18, 27), (9, 14))),
        (((1, 0), (4, 3), (7, 6), (2, 5), (8, 17), (16, 15), (14, None)), ((0, 9), (14, 18))),
    )
    core_0 = jnp.full((SLOT, LANES), core_ref[0], jnp.int32) == 0
    for core, (sides, ranges) in enumerate(places):
        for i in range(chips):
            a = mine_ref[SLOT * i : SLOT * (i + 1), :]
            b = other_ref[SLOT * i : SLOT * (i + 1), :]
            v = jnp.where(core_0, a, b) if core == 0 else jnp.where(core_0, b, a)
            rows_ref[CHUNK * i : CHUNK * (i + 1), :] = v[:CHUNK] * jnp.exp2(v[CHUNK : CHUNK + 1])
        for i, (lower, upper) in enumerate(sides):
            v = rows_ref[CH * i : CH * (i + 1), :]
            taps_ref[lower] = v[:, :CH]
            if upper is None:
                last_ref[...] = v[0:1, CH:]
                stores.append(pltpu.make_async_copy(last_ref, bias_ref, sems.at[len(stores)]))
                stores[-1].start()
            else:
                taps_ref[upper] = v[:, CH:]
        for first, end in ranges:
            part = pl.ds(first, end - first)
            stores.append(pltpu.make_async_copy(taps_ref.at[part], weight_ref.at[part], sems.at[len(stores)]))
            stores[-1].start()
    for store in stores:
        store.wait()


def in_vmem(array):
    return pltpu.with_memory_space_constraint(array, pltpu.VMEM)


def in_hbm(array):
    return pltpu.with_memory_space_constraint(array, pltpu.HBM)


def exchange(rows, axis):
    return in_vmem(lax.all_to_all(rows.reshape(-1, 1, LANES), axis, 0, 0, tiled=True).reshape(-1, LANES))


def exchange_slots(slots):
    return lax.all_to_all(slots.astype(jnp.float16), "chip", 0, 0, tiled=True)


def on_device(inputs, preact, grad_out, weight):
    chips = lax.axis_size("chip")
    slabs = chips * lax.axis_size("core")
    groups = lax.axis_size("rep")
    _, planes, height, packed = inputs.shape
    count = inputs.shape[0] * groups * planes * slabs * height * (packed // CH)
    scale = 1.0 / float(count) ** 0.5
    core = lax.axis_index("core").astype(jnp.int32).reshape(1)
    in_smem = pl.BlockSpec(memory_space=pltpu.SMEM)
    whole = pl.BlockSpec(memory_space=pltpu.VMEM)
    rows = height * packed // LANES
    own, pack = pl.pallas_call(
        mask_kernel,
        in_specs=[pl.BlockSpec(memory_space=pltpu.HBM)] * 3,
        out_shape=(
            pltpu.VMEM((height, packed), jnp.bfloat16),
            pltpu.VMEM((2 * height, packed), jnp.bfloat16),
        ),
        scratch_shapes=[pltpu.VMEM((height, packed), jnp.bfloat16)] * 2 + [pltpu.SemaphoreType.DMA((3,))],
        compiler_params=SMALL,
        name="mask",
    )(*(in_hbm(a.reshape(height, packed)) for a in (preact, grad_out, inputs)))
    swap = [(0, 1), (1, 0)]
    ends = range(1, slabs - 1, 2)
    far = lax.ppermute(own, ("chip", "core"), [(i, i + 1) for i in ends] + [(i + 1, i) for i in ends])
    near = in_vmem(lax.ppermute(pack, "core", swap))
    wt = pl.pallas_call(
        weights_kernel,
        in_specs=[in_smem, whole],
        out_shape=pltpu.VMEM((3 * LANES, 768), jnp.bfloat16),
        compiler_params=SMALL,
        name="weights",
    )(core, weight.reshape(27, CH, CH))

    def turned(pair):
        return pl.pallas_call(
            inputs_kernel,
            out_shape=pltpu.VMEM((3 * LANES, rows), jnp.bfloat16),
            compiler_params=SMALL,
            name="inputs",
        )(in_vmem(pair))

    dw, g = pl.pallas_call(
        kernel_gradient_kernel,
        in_specs=[in_smem] + [whole] * 5,
        out_shape=(
            pltpu.VMEM((chips * SLOT, LANES), jnp.float32),
            pltpu.VMEM((rows, 768), jnp.bfloat16),
        ),
        scratch_shapes=[pltpu.VMEM((chips * CHUNK, LANES), jnp.float32)],
        compiler_params=SMALL,
        name="kernel_gradient",
    )(core, in_vmem(far), in_vmem(own), near, in_vmem(turned(pack)), in_vmem(turned(near)))
    mine = pl.pallas_call(
        plane_sum_kernel,
        out_shape=pltpu.VMEM((groups * CHUNK, LANES), jnp.float32),
        compiler_params=SMALL,
        name="plane_sum",
    )(in_vmem(exchange_slots(dw).astype(jnp.float32)))
    total = pl.pallas_call(
        lambda p, o: finish_kernel(p, o, scale=scale),
        out_shape=pltpu.VMEM((chips * SLOT, LANES), jnp.float32),
        compiler_params=SMALL,
        name="finish",
    )(exchange(mine, "rep"))
    gathered = exchange_slots(total)
    other = lax.ppermute(gathered, "core", swap)
    dx = pl.pallas_call(
        input_gradient_kernel,
        out_shape=pltpu.VMEM((height, packed), jnp.bfloat16),
        compiler_params=SMALL,
        name="input_gradient",
    )(in_vmem(g), in_vmem(wt))
    weight_grad, bias_grad, dx = pl.pallas_call(
        unpack_kernel,
        in_specs=[in_smem, whole, whole, whole],
        out_specs=[pl.BlockSpec(memory_space=pltpu.HBM)] * 3,
        out_shape=(
            jax.ShapeDtypeStruct((27, CH, CH), jnp.float32),
            jax.ShapeDtypeStruct((1, CH), jnp.float32),
            jax.ShapeDtypeStruct((height, packed), jnp.bfloat16),
        ),
        scratch_shapes=[
            pltpu.VMEM((chips * CHUNK, LANES), jnp.float32),
            pltpu.VMEM((27, CH, CH), jnp.float32),
            pltpu.VMEM((1, CH), jnp.float32),
            pltpu.SemaphoreType.DMA((6,)),
        ],
        compiler_params=SMALL,
        name="unpack",
    )(core, in_vmem(gathered.astype(jnp.float32)), in_vmem(other.astype(jnp.float32)), in_vmem(dx))
    return dx.reshape(inputs.shape), weight_grad.reshape(3, 3, 3, CH, CH), bias_grad.reshape(CH)


def solution(mesh):
    groups, slabs = mesh.devices.shape
    by_core = jax.sharding.Mesh(mesh.devices.reshape(groups, slabs // 2, 2), ("rep", "chip", "core"))
    split = P("rep", ("chip", "core"), None, None)
    return jax.shard_map(
        on_device,
        mesh=by_core,
        in_specs=(split, split, split, P()),
        out_specs=(split, P(), P()),
        check_vma=False,
    )
```

```python
import jax
import jax.numpy as jnp
from jax import lax
from jax.experimental import pallas as pl
from jax.experimental.pallas import tpu as pltpu
from jax.sharding import PartitionSpec as P


CH = 64
LANES = 2 * CH
SLOT = 16
CHUNK = 14
SMALL = pltpu.CompilerParams(vmem_limit_bytes=16 * 1024 * 1024)


def mask_kernel(preact_ref, grad_ref, x_ref, own_ref, pack_ref, z_ref, dy_ref, sems):
    height = own_ref.shape[0]
    loads = (
        pltpu.make_async_copy(preact_ref, z_ref, sems.at[0]),
        pltpu.make_async_copy(grad_ref, dy_ref, sems.at[1]),
        pltpu.make_async_copy(x_ref, pack_ref.at[height:], sems.at[2]),
    )
    for load in loads:
        load.start()
    loads[0].wait()
    loads[1].wait()
    own = jnp.where(z_ref[...] > 0, dy_ref[...], jnp.zeros_like(dy_ref))
    own_ref[...] = own
    pack_ref[0:height, :] = own
    loads[2].wait()


def inputs_kernel(pair_ref, xt_ref):
    height, packed = pair_ref.shape[0] // 2, pair_ref.shape[1]
    x_ref = pair_ref.at[height:]
    pairs = packed // LANES
    rows = pairs * height
    x = jnp.concatenate([x_ref[:, LANES * j : LANES * (j + 1)] for j in range(pairs)], axis=0)
    xt = jnp.transpose(x.astype(jnp.float32))
    h = lax.broadcasted_iota(jnp.int32, (LANES, rows), 1) % height
    xt_ref[0:LANES, :] = jnp.where(h == 0, 0.0, pltpu.roll(xt, 1, 1)).astype(jnp.bfloat16)
    xt_ref[LANES : 2 * LANES, :] = xt.astype(jnp.bfloat16)
    xt_ref[2 * LANES :, :] = jnp.where(h == height - 1, 0.0, pltpu.roll(xt, rows - 1, 1)).astype(jnp.bfloat16)


def weights_kernel(core_ref, w_ref, wt_ref):
    core = core_ref[0]
    zero = jnp.zeros((CH, CH), jnp.bfloat16)
    for slot, od in enumerate((2 - 2 * core, 1, 2 * core)):
        for oh in range(3):
            t = 9 * od + 3 * oh
            before, here, after = w_ref[t], w_ref[t + 1], w_ref[t + 2]
            for parity in range(2):
                if parity == 0:
                    parts = (here, before, zero, after)
                else:
                    parts = (after, here, before, zero)
                r = (2 * oh + parity) * CH
                wt_ref[r : r + CH, 256 * slot : 256 * slot + LANES] = jnp.concatenate(parts[:2], axis=1)
                wt_ref[r : r + CH, 256 * slot + LANES : 256 * (slot + 1)] = jnp.concatenate(parts[2:], axis=1)


def kernel_gradient_kernel(core_ref, far_ref, own_ref, near_ref, xt_own_ref, xt_near_ref, slots_ref, g_ref, dw_ref):
    height, packed = own_ref.shape
    pairs = packed // LANES
    low = lax.broadcasted_iota(jnp.int32, (height, LANES), 1) < CH
    for slot, ref in enumerate((far_ref, own_ref, near_ref)):
        for j in range(pairs):
            at = slice(height * j, height * (j + 1))
            g_ref[at, 256 * slot : 256 * slot + LANES] = ref[0:height, LANES * j : LANES * (j + 1)]
            nothing = jnp.zeros((height, LANES), jnp.bfloat16)
            right = ref[0:height, LANES * (j + 1) : LANES * (j + 2)] if j + 1 < pairs else nothing
            left = ref[0:height, LANES * (j - 1) : LANES * j] if j > 0 else nothing
            g_ref[at, 256 * slot + LANES : 256 * (slot + 1)] = jnp.where(low, right, left)
    d = jnp.dot(xt_own_ref[...], g_ref[:, 0:512], preferred_element_type=jnp.float32)
    d = d + jnp.dot(xt_near_ref[...], g_ref[:, 256:768], preferred_element_type=jnp.float32)
    lo = lax.broadcasted_iota(jnp.int32, (CH, LANES), 1) < CH
    core_0 = jnp.full((CH, LANES), core_ref[0], jnp.int32) == 0

    def block(part, oh, parity, half):
        r = LANES * oh + CH * parity
        c = 256 * part + LANES * half
        return d[r : r + CH, c : c + LANES]

    def swap(v):
        return pltpu.roll(v, CH, 1)

    def two(part, oh):
        return block(part, oh, 0, 0) + jnp.where(lo, swap(block(part, oh, 1, 0)), swap(block(part, oh, 1, 1)))

    def low_one(part, oh):
        return block(part, oh, 1, 0) + swap(block(part, oh, 0, 1))

    def high_one(part, oh):
        return swap(block(part, oh, 1, 0)) + block(part, oh, 0, 1)

    total = jnp.sum(g_ref[:, 256:384].astype(jnp.float32) + g_ref[:, 512:640].astype(jnp.float32), axis=0, keepdims=True)
    first = lax.broadcasted_iota(jnp.int32, (CH, LANES), 0) == 0
    bias = jnp.where(first, jnp.broadcast_to(total + swap(total), (CH, LANES)), 0.0)
    blocks = (
        two(0, 0),
        two(0, 1),
        two(0, 2),
        jnp.where(lo, low_one(0, 0), high_one(0, 1)),
        jnp.where(lo, low_one(0, 2), jnp.where(core_0, high_one(1, 0), high_one(1, 2))),
        jnp.where(core_0, two(1, 0), two(1, 2)),
        jnp.where(core_0, two(1, 1), jnp.where(lo, low_one(1, 1), bias)),
    )
    largest = jnp.max(jnp.abs(blocks[0]), axis=0, keepdims=True)
    for v in blocks[1:]:
        largest = jnp.maximum(largest, jnp.max(jnp.abs(v), axis=0, keepdims=True))
    exponent = exponents(largest)
    unit = jnp.exp2(-exponent)
    for i, v in enumerate(blocks):
        dw_ref[CH * i : CH * (i + 1), :] = v * unit
    for i in range(slots_ref.shape[0] // SLOT):
        slots_ref[SLOT * i : SLOT * (i + 1), :] = to_slot(dw_ref[CHUNK * i : CHUNK * (i + 1), :], exponent)


def input_gradient_kernel(g_ref, wt_ref, dx_ref):
    height, packed = dx_ref.shape
    pairs = packed // LANES
    rows = pairs * height
    y = lax.dot_general(
        g_ref[...], wt_ref[...], (((1,), (1,)), ((), ())), preferred_element_type=jnp.float32
    )
    h = lax.broadcasted_iota(jnp.int32, (rows, LANES), 0) % height
    up = jnp.where(h == height - 1, 0.0, pltpu.roll(y[:, :LANES], rows - 1, 0))
    down = jnp.where(h == 0, 0.0, pltpu.roll(y[:, 2 * LANES :], 1, 0))
    out = (y[:, LANES : 2 * LANES] + up + down).astype(jnp.bfloat16)
    for j in range(pairs):
        dx_ref[:, LANES * j : LANES * (j + 1)] = out[height * j : height * (j + 1), :]


def exponents(largest):
    return jnp.floor(jnp.log2(jnp.maximum(largest, 1e-30))) - 14.0


def to_slot(rows, exponent):
    return jnp.concatenate([rows, exponent, jnp.zeros((SLOT - CHUNK - 1, LANES), jnp.float32)], axis=0)


def from_slot(slots_ref, i):
    unit = jnp.exp2(slots_ref[SLOT * i + CHUNK : SLOT * i + CHUNK + 1, :])
    return slots_ref[SLOT * i : SLOT * i + CHUNK, :] * unit


def sum_kernel(slots_ref, out_ref, *, scale):
    sums = [from_slot(slots_ref, i) for i in range(slots_ref.shape[0] // SLOT)]
    while len(sums) > 1:
        pairs = [a + b for a, b in zip(sums[::2], sums[1::2])]
        sums = pairs + sums[2 * len(pairs) :]
    s = sums[0] * scale
    exponent = exponents(jnp.max(jnp.abs(s), axis=0, keepdims=True))
    slot = to_slot(s * jnp.exp2(-exponent), exponent)
    for i in range(out_ref.shape[0] // SLOT):
        out_ref[SLOT * i : SLOT * (i + 1), :] = slot


def unpack_kernel(
    core_ref, mine_ref, other_ref, dx_ref, weight_ref, bias_ref, dx_out_ref, rows_ref, taps_ref, last_ref, sems
):
    stores = [pltpu.make_async_copy(dx_ref, dx_out_ref, sems.at[0])]
    stores[0].start()
    chips = mine_ref.shape[0] // SLOT
    places = (
        (((19, 18), (22, 21), (25, 24), (20, 23), (26, 11), (10, 9), (13, 12)), ((18, 27), (9, 14))),
        (((1, 0), (4, 3), (7, 6), (2, 5), (8, 17), (16, 15), (14, None)), ((0, 9), (14, 18))),
    )
    core_0 = jnp.full((SLOT, LANES), core_ref[0], jnp.int32) == 0
    for core, (sides, ranges) in enumerate(places):
        for i in range(chips):
            a = mine_ref[SLOT * i : SLOT * (i + 1), :]
            b = other_ref[SLOT * i : SLOT * (i + 1), :]
            v = jnp.where(core_0, a, b) if core == 0 else jnp.where(core_0, b, a)
            rows_ref[CHUNK * i : CHUNK * (i + 1), :] = v[:CHUNK] * jnp.exp2(v[CHUNK : CHUNK + 1])
        for i, (lower, upper) in enumerate(sides):
            v = rows_ref[CH * i : CH * (i + 1), :]
            taps_ref[lower] = v[:, :CH]
            if upper is None:
                last_ref[...] = v[0:1, CH:]
                stores.append(pltpu.make_async_copy(last_ref, bias_ref, sems.at[len(stores)]))
                stores[-1].start()
            else:
                taps_ref[upper] = v[:, CH:]
        for first, end in ranges:
            part = pl.ds(first, end - first)
            stores.append(pltpu.make_async_copy(taps_ref.at[part], weight_ref.at[part], sems.at[len(stores)]))
            stores[-1].start()
    for store in stores:
        store.wait()


def in_vmem(array):
    return pltpu.with_memory_space_constraint(array, pltpu.VMEM)


def in_hbm(array):
    return pltpu.with_memory_space_constraint(array, pltpu.HBM)


def exchange(slots, axis):
    return lax.all_to_all(slots.astype(jnp.float16), axis, 0, 0, tiled=True)


def sum_slots(slots, copies, scale):
    return pl.pallas_call(
        lambda s, o: sum_kernel(s, o, scale=scale),
        out_shape=pltpu.VMEM((copies * SLOT, LANES), jnp.float32),
        compiler_params=SMALL,
        name="sum_slots",
    )(in_vmem(slots.astype(jnp.float32)))


def on_device(inputs, preact, grad_out, weight):
    chips = lax.axis_size("chip")
    slabs = chips * lax.axis_size("core")
    groups = lax.axis_size("rep")
    _, planes, height, packed = inputs.shape
    count = inputs.shape[0] * groups * planes * slabs * height * (packed // CH)
    scale = 1.0 / float(count) ** 0.5
    core = lax.axis_index("core").astype(jnp.int32).reshape(1)
    in_smem = pl.BlockSpec(memory_space=pltpu.SMEM)
    whole = pl.BlockSpec(memory_space=pltpu.VMEM)
    rows = height * packed // LANES
    own, pack = pl.pallas_call(
        mask_kernel,
        in_specs=[pl.BlockSpec(memory_space=pltpu.HBM)] * 3,
        out_shape=(
            pltpu.VMEM((height, packed), jnp.bfloat16),
            pltpu.VMEM((2 * height, packed), jnp.bfloat16),
        ),
        scratch_shapes=[pltpu.VMEM((height, packed), jnp.bfloat16)] * 2 + [pltpu.SemaphoreType.DMA((3,))],
        compiler_params=SMALL,
        name="mask",
    )(*(in_hbm(a.reshape(height, packed)) for a in (preact, grad_out, inputs)))
    swap = [(0, 1), (1, 0)]
    ends = range(1, slabs - 1, 2)
    far = lax.ppermute(own, ("chip", "core"), [(i, i + 1) for i in ends] + [(i + 1, i) for i in ends])
    near = in_vmem(lax.ppermute(pack, "core", swap))
    wt = pl.pallas_call(
        weights_kernel,
        in_specs=[in_smem, whole],
        out_shape=pltpu.VMEM((3 * LANES, 768), jnp.bfloat16),
        compiler_params=SMALL,
        name="weights",
    )(core, weight.reshape(27, CH, CH))

    def turned(pair):
        return pl.pallas_call(
            inputs_kernel,
            out_shape=pltpu.VMEM((3 * LANES, rows), jnp.bfloat16),
            compiler_params=SMALL,
            name="inputs",
        )(in_vmem(pair))

    dw, g = pl.pallas_call(
        kernel_gradient_kernel,
        in_specs=[in_smem] + [whole] * 5,
        out_shape=(
            pltpu.VMEM((chips * SLOT, LANES), jnp.float32),
            pltpu.VMEM((rows, 768), jnp.bfloat16),
        ),
        scratch_shapes=[pltpu.VMEM((chips * CHUNK, LANES), jnp.float32)],
        compiler_params=SMALL,
        name="kernel_gradient",
    )(core, in_vmem(far), in_vmem(own), near, in_vmem(turned(pack)), in_vmem(turned(near)))
    mine = sum_slots(exchange(dw, "chip"), groups, 1.0)
    total = sum_slots(exchange(mine, "rep"), chips, scale)
    gathered = exchange(total, "chip")
    other = lax.ppermute(gathered, "core", swap)
    dx = pl.pallas_call(
        input_gradient_kernel,
        out_shape=pltpu.VMEM((height, packed), jnp.bfloat16),
        compiler_params=SMALL,
        name="input_gradient",
    )(in_vmem(g), in_vmem(wt))
    weight_grad, bias_grad, dx = pl.pallas_call(
        unpack_kernel,
        in_specs=[in_smem, whole, whole, whole],
        out_specs=[pl.BlockSpec(memory_space=pltpu.HBM)] * 3,
        out_shape=(
            jax.ShapeDtypeStruct((27, CH, CH), jnp.float32),
            jax.ShapeDtypeStruct((1, CH), jnp.float32),
            jax.ShapeDtypeStruct((height, packed), jnp.bfloat16),
        ),
        scratch_shapes=[
            pltpu.VMEM((chips * CHUNK, LANES), jnp.float32),
            pltpu.VMEM((27, CH, CH), jnp.float32),
            pltpu.VMEM((1, CH), jnp.float32),
            pltpu.SemaphoreType.DMA((6,)),
        ],
        compiler_params=SMALL,
        name="unpack",
    )(core, in_vmem(gathered.astype(jnp.float32)), in_vmem(other.astype(jnp.float32)), in_vmem(dx))
    return dx.reshape(inputs.shape), weight_grad.reshape(3, 3, 3, CH, CH), bias_grad.reshape(CH)


def solution(mesh):
    groups, slabs = mesh.devices.shape
    by_core = jax.sharding.Mesh(mesh.devices.reshape(groups, slabs // 2, 2), ("rep", "chip", "core"))
    split = P("rep", ("chip", "core"), None, None)
    return jax.shard_map(
        on_device,
        mesh=by_core,
        in_specs=(split, split, split, P()),
        out_specs=(split, P(), P()),
        check_vma=False,
    )
```

```python
import jax
import jax.numpy as jnp
from jax import lax
from jax.experimental import pallas as pl
from jax.experimental.pallas import tpu as pltpu
from jax.sharding import PartitionSpec as P


CH = 64
LANES = 2 * CH
SLOT = 16
CHUNK = 14
SMALL = pltpu.CompilerParams(vmem_limit_bytes=16 * 1024 * 1024)


def mask_kernel(preact_ref, grad_ref, x_ref, own_ref, pack_ref, z_ref, dy_ref, sems):
    height = own_ref.shape[0]
    loads = (
        pltpu.make_async_copy(preact_ref, z_ref, sems.at[0]),
        pltpu.make_async_copy(grad_ref, dy_ref, sems.at[1]),
        pltpu.make_async_copy(x_ref, pack_ref.at[height:], sems.at[2]),
    )
    for load in loads:
        load.start()
    loads[0].wait()
    loads[1].wait()
    own = jnp.where(z_ref[...] > 0, dy_ref[...], jnp.zeros_like(dy_ref))
    own_ref[...] = own
    pack_ref[0:height, :] = own
    loads[2].wait()


def inputs_kernel(pair_ref, xt_ref):
    height, packed = pair_ref.shape[0] // 2, pair_ref.shape[1]
    x_ref = pair_ref.at[height:]
    pairs = packed // LANES
    rows = pairs * height
    x = jnp.concatenate([x_ref[:, LANES * j : LANES * (j + 1)] for j in range(pairs)], axis=0)
    xt = jnp.transpose(x.astype(jnp.float32))
    h = lax.broadcasted_iota(jnp.int32, (LANES, rows), 1) % height
    xt_ref[0:LANES, :] = jnp.where(h == 0, 0.0, pltpu.roll(xt, 1, 1)).astype(jnp.bfloat16)
    xt_ref[LANES : 2 * LANES, :] = xt.astype(jnp.bfloat16)
    xt_ref[2 * LANES :, :] = jnp.where(h == height - 1, 0.0, pltpu.roll(xt, rows - 1, 1)).astype(jnp.bfloat16)


def weights_kernel(core_ref, w_ref, wt_ref):
    core = core_ref[0]
    zero = jnp.zeros((CH, CH), jnp.bfloat16)
    for slot, od in enumerate((2 - 2 * core, 1, 2 * core)):
        for oh in range(3):
            t = 9 * od + 3 * oh
            before, here, after = w_ref[t], w_ref[t + 1], w_ref[t + 2]
            for parity in range(2):
                if parity == 0:
                    parts = (here, before, zero, after)
                else:
                    parts = (after, here, before, zero)
                r = (2 * oh + parity) * CH
                wt_ref[r : r + CH, 256 * slot : 256 * slot + LANES] = jnp.concatenate(parts[:2], axis=1)
                wt_ref[r : r + CH, 256 * slot + LANES : 256 * (slot + 1)] = jnp.concatenate(parts[2:], axis=1)


def lay_out(ref, g_ref, column):
    height, packed = g_ref.shape[0] * LANES // ref.shape[1], ref.shape[1]
    pairs = packed // LANES
    low = lax.broadcasted_iota(jnp.int32, (height, LANES), 1) < CH
    nothing = jnp.zeros((height, LANES), jnp.bfloat16)
    for j in range(pairs):
        at = slice(height * j, height * (j + 1))
        g_ref[at, column : column + LANES] = ref[0:height, LANES * j : LANES * (j + 1)]
        right = ref[0:height, LANES * (j + 1) : LANES * (j + 2)] if j + 1 < pairs else nothing
        left = ref[0:height, LANES * (j - 1) : LANES * j] if j > 0 else nothing
        g_ref[at, column + LANES : column + 256] = jnp.where(low, right, left)


def own_planes_kernel(own_ref, near_ref, xt_own_ref, xt_near_ref, d_ref, g_ref):
    lay_out(own_ref, g_ref, 0)
    lay_out(near_ref, g_ref, 256)
    d = jnp.dot(xt_near_ref[...], g_ref[...], preferred_element_type=jnp.float32)
    own = jnp.dot(xt_own_ref[...], g_ref[:, 0:256], preferred_element_type=jnp.float32)
    d_ref[:, 0:256] = d[:, 0:256]
    d_ref[:, 256:512] = d[:, 256:512] + own


def kernel_gradient_kernel(core_ref, far_ref, g_ref, xt_own_ref, d_ref, slots_ref, g_far_ref, dw_ref):
    lay_out(far_ref, g_far_ref, 0)
    parts = (
        d_ref[:, 0:256] + jnp.dot(xt_own_ref[...], g_far_ref[...], preferred_element_type=jnp.float32),
        d_ref[:, 256:512],
    )
    lo = lax.broadcasted_iota(jnp.int32, (CH, LANES), 1) < CH
    core_0 = jnp.full((CH, LANES), core_ref[0], jnp.int32) == 0

    def block(part, oh, parity, half):
        r = LANES * oh + CH * parity
        return parts[part][r : r + CH, LANES * half : LANES * (half + 1)]

    def swap(v):
        return pltpu.roll(v, CH, 1)

    def two(part, oh):
        return block(part, oh, 0, 0) + jnp.where(lo, swap(block(part, oh, 1, 0)), swap(block(part, oh, 1, 1)))

    def low_one(part, oh):
        return block(part, oh, 1, 0) + swap(block(part, oh, 0, 1))

    def high_one(part, oh):
        return swap(block(part, oh, 1, 0)) + block(part, oh, 0, 1)

    total = jnp.sum(g_ref[:, 0:128].astype(jnp.float32) + g_ref[:, 256:384].astype(jnp.float32), axis=0, keepdims=True)
    first = lax.broadcasted_iota(jnp.int32, (CH, LANES), 0) == 0
    bias = jnp.where(first, jnp.broadcast_to(total + swap(total), (CH, LANES)), 0.0)
    blocks = (
        two(0, 0),
        two(0, 1),
        two(0, 2),
        jnp.where(lo, low_one(0, 0), high_one(0, 1)),
        jnp.where(lo, low_one(0, 2), jnp.where(core_0, high_one(1, 0), high_one(1, 2))),
        jnp.where(core_0, two(1, 0), two(1, 2)),
        jnp.where(core_0, two(1, 1), jnp.where(lo, low_one(1, 1), bias)),
    )
    largest = jnp.max(jnp.abs(blocks[0]), axis=0, keepdims=True)
    for v in blocks[1:]:
        largest = jnp.maximum(largest, jnp.max(jnp.abs(v), axis=0, keepdims=True))
    exponent = exponents(largest)
    unit = jnp.exp2(-exponent)
    for i, v in enumerate(blocks):
        dw_ref[CH * i : CH * (i + 1), :] = v * unit
    for i in range(slots_ref.shape[0] // SLOT):
        slots_ref[SLOT * i : SLOT * (i + 1), :] = to_slot(dw_ref[CHUNK * i : CHUNK * (i + 1), :], exponent)


def input_gradient_kernel(g_far_ref, g_ref, wt_ref, dx_ref):
    height, packed = dx_ref.shape
    pairs = packed // LANES
    rows = pairs * height
    turn = (((1,), (1,)), ((), ()))
    y = lax.dot_general(g_ref[...], wt_ref[:, 256:768], turn, preferred_element_type=jnp.float32)
    y = y + lax.dot_general(g_far_ref[...], wt_ref[:, 0:256], turn, preferred_element_type=jnp.float32)
    h = lax.broadcasted_iota(jnp.int32, (rows, LANES), 0) % height
    up = jnp.where(h == height - 1, 0.0, pltpu.roll(y[:, :LANES], rows - 1, 0))
    down = jnp.where(h == 0, 0.0, pltpu.roll(y[:, 2 * LANES :], 1, 0))
    out = (y[:, LANES : 2 * LANES] + up + down).astype(jnp.bfloat16)
    for j in range(pairs):
        dx_ref[:, LANES * j : LANES * (j + 1)] = out[height * j : height * (j + 1), :]


def exponents(largest):
    return jnp.floor(jnp.log2(jnp.maximum(largest, 1e-30))) - 14.0


def to_slot(rows, exponent):
    return jnp.concatenate([rows, exponent, jnp.zeros((SLOT - CHUNK - 1, LANES), jnp.float32)], axis=0)


def from_slot(slots_ref, i):
    unit = jnp.exp2(slots_ref[SLOT * i + CHUNK : SLOT * i + CHUNK + 1, :])
    return slots_ref[SLOT * i : SLOT * i + CHUNK, :] * unit


def plane_sum_kernel(slots_ref, out_ref):
    sums = [from_slot(slots_ref, i) for i in range(slots_ref.shape[0] // SLOT)]
    while len(sums) > 1:
        sums = [a + b for a, b in zip(sums[::2], sums[1::2], strict=True)]
    for i in range(out_ref.shape[0] // CHUNK):
        out_ref[CHUNK * i : CHUNK * (i + 1), :] = sums[0]


def finish_kernel(parts_ref, out_ref, *, scale):
    s = parts_ref[0:CHUNK, :]
    for i in range(1, parts_ref.shape[0] // CHUNK):
        s = s + parts_ref[CHUNK * i : CHUNK * (i + 1), :]
    s = s * scale
    exponent = exponents(jnp.max(jnp.abs(s), axis=0, keepdims=True))
    slot = to_slot(s * jnp.exp2(-exponent), exponent)
    for i in range(out_ref.shape[0] // SLOT):
        out_ref[SLOT * i : SLOT * (i + 1), :] = slot


PLACES = (
    (((19, 18), (22, 21), (25, 24), (20, 23), (26, 11), (10, 9), (13, 12)), ((18, 27), (9, 14))),
    (((1, 0), (4, 3), (7, 6), (2, 5), (8, 17), (16, 15), (14, None)), ((0, 9), (14, 18))),
)


def unpack_half(half, slots_ref, weight_ref, bias_ref, rows_ref, taps_ref, last_ref, sems):
    sides, ranges = PLACES[half]
    for i in range(slots_ref.shape[0] // SLOT):
        rows_ref[CHUNK * i : CHUNK * (i + 1), :] = from_slot(slots_ref, i)
    stores = []
    for i, (lower, upper) in enumerate(sides):
        v = rows_ref[CH * i : CH * (i + 1), :]
        taps_ref[lower] = v[:, :CH]
        if upper is None:
            last_ref[...] = v[0:1, CH:]
            stores.append(pltpu.make_async_copy(last_ref, bias_ref, sems.at[2]))
        else:
            taps_ref[upper] = v[:, CH:]
    for i, (first, end) in enumerate(ranges):
        part = pl.ds(first, end - first)
        stores.append(pltpu.make_async_copy(taps_ref.at[part], weight_ref.at[part], sems.at[i]))
    for store in stores:
        store.start()
    for store in stores:
        store.wait()


def unpack_mine_kernel(core_ref, slots_ref, dx_ref, weight_ref, bias_ref, dx_out_ref, *scratch):
    sems = scratch[-1]
    dx_store = pltpu.make_async_copy(dx_ref, dx_out_ref, sems.at[3])
    dx_store.start()
    for half in range(2):

        @pl.when(core_ref[0] == half)
        def _():
            unpack_half(half, slots_ref, weight_ref, bias_ref, *scratch)

    dx_store.wait()


def unpack_other_kernel(core_ref, slots_ref, _weight_ref, _bias_ref, weight_ref, bias_ref, *scratch):
    for half in range(2):

        @pl.when(core_ref[0] == 1 - half)
        def _():
            unpack_half(half, slots_ref, weight_ref, bias_ref, *scratch)


def in_vmem(array):
    return pltpu.with_memory_space_constraint(array, pltpu.VMEM)


def in_hbm(array):
    return pltpu.with_memory_space_constraint(array, pltpu.HBM)


def exchange(rows, axis):
    return in_vmem(lax.all_to_all(rows.reshape(-1, 1, LANES), axis, 0, 0, tiled=True).reshape(-1, LANES))


def exchange_slots(slots):
    return lax.all_to_all(slots.astype(jnp.float16), "chip", 0, 0, tiled=True)


def on_device(inputs, preact, grad_out, weight):
    chips = lax.axis_size("chip")
    slabs = chips * lax.axis_size("core")
    groups = lax.axis_size("rep")
    _, planes, height, packed = inputs.shape
    count = inputs.shape[0] * groups * planes * slabs * height * (packed // CH)
    scale = 1.0 / float(count) ** 0.5
    core = lax.axis_index("core").astype(jnp.int32).reshape(1)
    in_smem = pl.BlockSpec(memory_space=pltpu.SMEM)
    whole = pl.BlockSpec(memory_space=pltpu.VMEM)
    rows = height * packed // LANES
    own, pack = pl.pallas_call(
        mask_kernel,
        in_specs=[pl.BlockSpec(memory_space=pltpu.HBM)] * 3,
        out_shape=(
            pltpu.VMEM((height, packed), jnp.bfloat16),
            pltpu.VMEM((2 * height, packed), jnp.bfloat16),
        ),
        scratch_shapes=[pltpu.VMEM((height, packed), jnp.bfloat16)] * 2 + [pltpu.SemaphoreType.DMA((3,))],
        compiler_params=SMALL,
        name="mask",
    )(*(in_hbm(a.reshape(height, packed)) for a in (preact, grad_out, inputs)))
    swap = [(0, 1), (1, 0)]
    ends = range(1, slabs - 1, 2)
    far = lax.ppermute(own, ("chip", "core"), [(i, i + 1) for i in ends] + [(i + 1, i) for i in ends])
    near = in_vmem(lax.ppermute(pack, "core", swap))
    wt = pl.pallas_call(
        weights_kernel,
        in_specs=[in_smem, whole],
        out_shape=pltpu.VMEM((3 * LANES, 768), jnp.bfloat16),
        compiler_params=SMALL,
        name="weights",
    )(core, weight.reshape(27, CH, CH))

    def turned(pair):
        return pl.pallas_call(
            inputs_kernel,
            out_shape=pltpu.VMEM((3 * LANES, rows), jnp.bfloat16),
            compiler_params=SMALL,
            name="inputs",
        )(in_vmem(pair))

    xt_own = in_vmem(turned(pack))
    d, g = pl.pallas_call(
        own_planes_kernel,
        out_shape=(
            pltpu.VMEM((3 * LANES, 512), jnp.float32),
            pltpu.VMEM((rows, 512), jnp.bfloat16),
        ),
        compiler_params=SMALL,
        name="own_planes",
    )(in_vmem(own), near, xt_own, in_vmem(turned(near)))
    dw, g_far = pl.pallas_call(
        kernel_gradient_kernel,
        in_specs=[in_smem] + [whole] * 4,
        out_shape=(
            pltpu.VMEM((chips * SLOT, LANES), jnp.float32),
            pltpu.VMEM((rows, 256), jnp.bfloat16),
        ),
        scratch_shapes=[pltpu.VMEM((chips * CHUNK, LANES), jnp.float32)],
        compiler_params=SMALL,
        name="kernel_gradient",
    )(core, in_vmem(far), in_vmem(g), xt_own, in_vmem(d))
    mine = pl.pallas_call(
        plane_sum_kernel,
        out_shape=pltpu.VMEM((groups * CHUNK, LANES), jnp.float32),
        compiler_params=SMALL,
        name="plane_sum",
    )(in_vmem(exchange_slots(dw).astype(jnp.float32)))
    total = pl.pallas_call(
        lambda p, o: finish_kernel(p, o, scale=scale),
        out_shape=pltpu.VMEM((chips * SLOT, LANES), jnp.float32),
        compiler_params=SMALL,
        name="finish",
    )(exchange(mine, "rep"))
    gathered = exchange_slots(total)
    hbm = pl.BlockSpec(memory_space=pltpu.HBM)
    grads = (
        jax.ShapeDtypeStruct((27, CH, CH), jnp.float32),
        jax.ShapeDtypeStruct((1, CH), jnp.float32),
    )
    scratch = [
        pltpu.VMEM((chips * CHUNK, LANES), jnp.float32),
        pltpu.VMEM((27, CH, CH), jnp.float32),
        pltpu.VMEM((1, CH), jnp.float32),
        pltpu.SemaphoreType.DMA((4,)),
    ]
    other = lax.ppermute(gathered, "core", swap)
    dx = pl.pallas_call(
        input_gradient_kernel,
        out_shape=pltpu.VMEM((height, packed), jnp.bfloat16),
        compiler_params=SMALL,
        name="input_gradient",
    )(in_vmem(g_far), in_vmem(g), in_vmem(wt))
    weight_grad, bias_grad, dx = pl.pallas_call(
        unpack_mine_kernel,
        in_specs=[in_smem, whole, whole],
        out_specs=[hbm] * 3,
        out_shape=grads + (jax.ShapeDtypeStruct((height, packed), jnp.bfloat16),),
        scratch_shapes=scratch,
        compiler_params=SMALL,
        name="unpack_mine",
    )(core, in_vmem(gathered.astype(jnp.float32)), in_vmem(dx))
    weight_grad, bias_grad = pl.pallas_call(
        unpack_other_kernel,
        in_specs=[in_smem, whole, hbm, hbm],
        out_specs=[hbm] * 2,
        out_shape=grads,
        scratch_shapes=scratch,
        input_output_aliases={2: 0, 3: 1},
        compiler_params=SMALL,
        name="unpack_other",
    )(core, in_vmem(other.astype(jnp.float32)), weight_grad, bias_grad)
    return dx.reshape(inputs.shape), weight_grad.reshape(3, 3, 3, CH, CH), bias_grad.reshape(CH)


def solution(mesh):
    groups, slabs = mesh.devices.shape
    by_core = jax.sharding.Mesh(mesh.devices.reshape(groups, slabs // 2, 2), ("rep", "chip", "core"))
    split = P("rep", ("chip", "core"), None, None)
    return jax.shard_map(
        on_device,
        mesh=by_core,
        in_specs=(split, split, split, P()),
        out_specs=(split, P(), P()),
        check_vma=False,
    )
```

```python
import jax
import jax.numpy as jnp
from jax import lax
from jax.experimental import pallas as pl
from jax.experimental.pallas import tpu as pltpu
from jax.sharding import PartitionSpec as P


CH = 64
LANES = 2 * CH
SLOT = 16
CHUNK = 14
SMALL = pltpu.CompilerParams(vmem_limit_bytes=16 * 1024 * 1024)


def mask_kernel(preact_ref, grad_ref, x_ref, own_ref, pack_ref, z_ref, dy_ref, sems):
    height = own_ref.shape[0]
    loads = (
        pltpu.make_async_copy(preact_ref, z_ref, sems.at[0]),
        pltpu.make_async_copy(grad_ref, dy_ref, sems.at[1]),
        pltpu.make_async_copy(x_ref, pack_ref.at[height:], sems.at[2]),
    )
    for load in loads:
        load.start()
    loads[0].wait()
    loads[1].wait()
    own = jnp.where(z_ref[...] > 0, dy_ref[...], jnp.zeros_like(dy_ref))
    own_ref[...] = own
    pack_ref[0:height, :] = own
    loads[2].wait()


def inputs_kernel(pair_ref, xt_ref):
    height, packed = pair_ref.shape[0] // 2, pair_ref.shape[1]
    x_ref = pair_ref.at[height:]
    pairs = packed // LANES
    rows = pairs * height
    x = jnp.concatenate([x_ref[:, LANES * j : LANES * (j + 1)] for j in range(pairs)], axis=0)
    xt = jnp.transpose(x.astype(jnp.float32))
    h = lax.broadcasted_iota(jnp.int32, (LANES, rows), 1) % height
    xt_ref[0:LANES, :] = jnp.where(h == 0, 0.0, pltpu.roll(xt, 1, 1)).astype(jnp.bfloat16)
    xt_ref[LANES : 2 * LANES, :] = xt.astype(jnp.bfloat16)
    xt_ref[2 * LANES :, :] = jnp.where(h == height - 1, 0.0, pltpu.roll(xt, rows - 1, 1)).astype(jnp.bfloat16)


def weights_kernel(core_ref, w_ref, wt_ref):
    core = core_ref[0]
    zero = jnp.zeros((CH, CH), jnp.bfloat16)
    for slot, od in enumerate((2 - 2 * core, 1, 2 * core)):
        for oh in range(3):
            t = 9 * od + 3 * oh
            before, here, after = w_ref[t], w_ref[t + 1], w_ref[t + 2]
            for parity in range(2):
                if parity == 0:
                    parts = (here, before, zero, after)
                else:
                    parts = (after, here, before, zero)
                r = (2 * oh + parity) * CH
                wt_ref[r : r + CH, 256 * slot : 256 * slot + LANES] = jnp.concatenate(parts[:2], axis=1)
                wt_ref[r : r + CH, 256 * slot + LANES : 256 * (slot + 1)] = jnp.concatenate(parts[2:], axis=1)


def lay_out(ref, g_ref, column):
    height, packed = g_ref.shape[0] * LANES // ref.shape[1], ref.shape[1]
    pairs = packed // LANES
    low = lax.broadcasted_iota(jnp.int32, (height, LANES), 1) < CH
    nothing = jnp.zeros((height, LANES), jnp.bfloat16)
    for j in range(pairs):
        at = slice(height * j, height * (j + 1))
        g_ref[at, column : column + LANES] = ref[0:height, LANES * j : LANES * (j + 1)]
        right = ref[0:height, LANES * (j + 1) : LANES * (j + 2)] if j + 1 < pairs else nothing
        left = ref[0:height, LANES * (j - 1) : LANES * j] if j > 0 else nothing
        g_ref[at, column + LANES : column + 256] = jnp.where(low, right, left)


def own_planes_kernel(own_ref, near_ref, xt_own_ref, xt_near_ref, d_ref, g_ref):
    lay_out(own_ref, g_ref, 0)
    lay_out(near_ref, g_ref, 256)
    d = jnp.dot(xt_near_ref[...], g_ref[...], preferred_element_type=jnp.float32)
    own = jnp.dot(xt_own_ref[...], g_ref[:, 0:256], preferred_element_type=jnp.float32)
    d_ref[:, 0:256] = d[:, 0:256]
    d_ref[:, 256:512] = d[:, 256:512] + own


def kernel_gradient_kernel(core_ref, far_ref, g_ref, xt_own_ref, d_ref, slots_ref, g_far_ref, dw_ref):
    lay_out(far_ref, g_far_ref, 0)
    parts = (
        d_ref[:, 0:256] + jnp.dot(xt_own_ref[...], g_far_ref[...], preferred_element_type=jnp.float32),
        d_ref[:, 256:512],
    )
    lo = lax.broadcasted_iota(jnp.int32, (CH, LANES), 1) < CH
    core_0 = jnp.full((CH, LANES), core_ref[0], jnp.int32) == 0

    def block(part, oh, parity, half):
        r = LANES * oh + CH * parity
        return parts[part][r : r + CH, LANES * half : LANES * (half + 1)]

    def swap(v):
        return pltpu.roll(v, CH, 1)

    def two(part, oh):
        return block(part, oh, 0, 0) + jnp.where(lo, swap(block(part, oh, 1, 0)), swap(block(part, oh, 1, 1)))

    def low_one(part, oh):
        return block(part, oh, 1, 0) + swap(block(part, oh, 0, 1))

    def high_one(part, oh):
        return swap(block(part, oh, 1, 0)) + block(part, oh, 0, 1)

    total = jnp.sum(g_ref[:, 0:128].astype(jnp.float32) + g_ref[:, 256:384].astype(jnp.float32), axis=0, keepdims=True)
    first = lax.broadcasted_iota(jnp.int32, (CH, LANES), 0) == 0
    bias = jnp.where(first, jnp.broadcast_to(total + swap(total), (CH, LANES)), 0.0)
    blocks = (
        two(0, 0),
        two(0, 1),
        two(0, 2),
        jnp.where(lo, low_one(0, 0), high_one(0, 1)),
        jnp.where(lo, low_one(0, 2), jnp.where(core_0, high_one(1, 0), high_one(1, 2))),
        jnp.where(core_0, two(1, 0), two(1, 2)),
        jnp.where(core_0, two(1, 1), jnp.where(lo, low_one(1, 1), bias)),
    )
    largest = jnp.max(jnp.abs(blocks[0]), axis=0, keepdims=True)
    for v in blocks[1:]:
        largest = jnp.maximum(largest, jnp.max(jnp.abs(v), axis=0, keepdims=True))
    exponent = exponents(largest)
    unit = jnp.exp2(-exponent)
    for i, v in enumerate(blocks):
        dw_ref[CH * i : CH * (i + 1), :] = v * unit
    for i in range(slots_ref.shape[0] // SLOT):
        slots_ref[SLOT * i : SLOT * (i + 1), :] = to_slot(dw_ref[CHUNK * i : CHUNK * (i + 1), :], exponent)


def input_gradient_kernel(g_far_ref, g_ref, wt_ref, dx_ref):
    height, packed = dx_ref.shape
    pairs = packed // LANES
    rows = pairs * height
    turn = (((1,), (1,)), ((), ()))
    y = lax.dot_general(g_ref[...], wt_ref[:, 256:768], turn, preferred_element_type=jnp.float32)
    y = y + lax.dot_general(g_far_ref[...], wt_ref[:, 0:256], turn, preferred_element_type=jnp.float32)
    h = lax.broadcasted_iota(jnp.int32, (rows, LANES), 0) % height
    up = jnp.where(h == height - 1, 0.0, pltpu.roll(y[:, :LANES], rows - 1, 0))
    down = jnp.where(h == 0, 0.0, pltpu.roll(y[:, 2 * LANES :], 1, 0))
    out = (y[:, LANES : 2 * LANES] + up + down).astype(jnp.bfloat16)
    for j in range(pairs):
        dx_ref[:, LANES * j : LANES * (j + 1)] = out[height * j : height * (j + 1), :]


def exponents(largest):
    return jnp.floor(jnp.log2(jnp.maximum(largest, 1e-30))) - 14.0


def to_slot(rows, exponent):
    return jnp.concatenate([rows, exponent, jnp.zeros((SLOT - CHUNK - 1, LANES), jnp.float32)], axis=0)


def from_slot(slots_ref, i):
    unit = jnp.exp2(slots_ref[SLOT * i + CHUNK : SLOT * i + CHUNK + 1, :])
    return slots_ref[SLOT * i : SLOT * i + CHUNK, :] * unit


def plane_sum_kernel(slots_ref, out_ref):
    sums = [from_slot(slots_ref, i) for i in range(slots_ref.shape[0] // SLOT)]
    while len(sums) > 1:
        sums = [a + b for a, b in zip(sums[::2], sums[1::2], strict=True)]
    for i in range(out_ref.shape[0] // CHUNK):
        out_ref[CHUNK * i : CHUNK * (i + 1), :] = sums[0]


def finish_kernel(parts_ref, out_ref, *, scale):
    s = parts_ref[0:CHUNK, :]
    for i in range(1, parts_ref.shape[0] // CHUNK):
        s = s + parts_ref[CHUNK * i : CHUNK * (i + 1), :]
    s = s * scale
    exponent = exponents(jnp.max(jnp.abs(s), axis=0, keepdims=True))
    slot = to_slot(s * jnp.exp2(-exponent), exponent)
    for i in range(out_ref.shape[0] // SLOT):
        out_ref[SLOT * i : SLOT * (i + 1), :] = slot


def unpack_kernel(
    core_ref, mine_ref, other_ref, dx_ref, weight_ref, bias_ref, dx_out_ref, rows_ref, taps_ref, last_ref, sems
):
    stores = [pltpu.make_async_copy(dx_ref, dx_out_ref, sems.at[0])]
    stores[0].start()
    chips = mine_ref.shape[0] // SLOT
    places = (
        (((19, 18), (22, 21), (25, 24), (20, 23), (26, 11), (10, 9), (13, 12)), ((18, 27), (9, 14))),
        (((1, 0), (4, 3), (7, 6), (2, 5), (8, 17), (16, 15), (14, None)), ((0, 9), (14, 18))),
    )
    core_0 = jnp.full((SLOT, LANES), core_ref[0], jnp.int32) == 0
    for core, (sides, ranges) in enumerate(places):
        for i in range(chips):
            a = mine_ref[SLOT * i : SLOT * (i + 1), :]
            b = other_ref[SLOT * i : SLOT * (i + 1), :]
            v = jnp.where(core_0, a, b) if core == 0 else jnp.where(core_0, b, a)
            rows_ref[CHUNK * i : CHUNK * (i + 1), :] = v[:CHUNK] * jnp.exp2(v[CHUNK : CHUNK + 1])
        for i, (lower, upper) in enumerate(sides):
            v = rows_ref[CH * i : CH * (i + 1), :]
            taps_ref[lower] = v[:, :CH]
            if upper is None:
                last_ref[...] = v[0:1, CH:]
                stores.append(pltpu.make_async_copy(last_ref, bias_ref, sems.at[len(stores)]))
                stores[-1].start()
            else:
                taps_ref[upper] = v[:, CH:]
        for first, end in ranges:
            part = pl.ds(first, end - first)
            stores.append(pltpu.make_async_copy(taps_ref.at[part], weight_ref.at[part], sems.at[len(stores)]))
            stores[-1].start()
    for store in stores:
        store.wait()


def in_vmem(array):
    return pltpu.with_memory_space_constraint(array, pltpu.VMEM)


def in_hbm(array):
    return pltpu.with_memory_space_constraint(array, pltpu.HBM)


def exchange(rows, axis):
    return in_vmem(lax.all_to_all(rows.reshape(-1, 1, LANES), axis, 0, 0, tiled=True).reshape(-1, LANES))


def exchange_slots(slots):
    return lax.all_to_all(slots.astype(jnp.float16), "chip", 0, 0, tiled=True)


def on_device(inputs, preact, grad_out, weight):
    chips = lax.axis_size("chip")
    slabs = chips * lax.axis_size("core")
    groups = lax.axis_size("rep")
    _, planes, height, packed = inputs.shape
    count = inputs.shape[0] * groups * planes * slabs * height * (packed // CH)
    scale = 1.0 / float(count) ** 0.5
    core = lax.axis_index("core").astype(jnp.int32).reshape(1)
    in_smem = pl.BlockSpec(memory_space=pltpu.SMEM)
    whole = pl.BlockSpec(memory_space=pltpu.VMEM)
    rows = height * packed // LANES
    own, pack = pl.pallas_call(
        mask_kernel,
        in_specs=[pl.BlockSpec(memory_space=pltpu.HBM)] * 3,
        out_shape=(
            pltpu.VMEM((height, packed), jnp.bfloat16),
            pltpu.VMEM((2 * height, packed), jnp.bfloat16),
        ),
        scratch_shapes=[pltpu.VMEM((height, packed), jnp.bfloat16)] * 2 + [pltpu.SemaphoreType.DMA((3,))],
        compiler_params=SMALL,
        name="mask",
    )(*(in_hbm(a.reshape(height, packed)) for a in (preact, grad_out, inputs)))
    swap = [(0, 1), (1, 0)]
    ends = range(1, slabs - 1, 2)
    far = lax.ppermute(own, ("chip", "core"), [(i, i + 1) for i in ends] + [(i + 1, i) for i in ends])
    near = in_vmem(lax.ppermute(pack, "core", swap))
    wt = pl.pallas_call(
        weights_kernel,
        in_specs=[in_smem, whole],
        out_shape=pltpu.VMEM((3 * LANES, 768), jnp.bfloat16),
        compiler_params=SMALL,
        name="weights",
    )(core, weight.reshape(27, CH, CH))

    def turned(pair):
        return pl.pallas_call(
            inputs_kernel,
            out_shape=pltpu.VMEM((3 * LANES, rows), jnp.bfloat16),
            compiler_params=SMALL,
            name="inputs",
        )(in_vmem(pair))

    xt_own = in_vmem(turned(pack))
    d, g = pl.pallas_call(
        own_planes_kernel,
        out_shape=(
            pltpu.VMEM((3 * LANES, 512), jnp.float32),
            pltpu.VMEM((rows, 512), jnp.bfloat16),
        ),
        compiler_params=SMALL,
        name="own_planes",
    )(in_vmem(own), near, xt_own, in_vmem(turned(near)))
    dw, g_far = pl.pallas_call(
        kernel_gradient_kernel,
        in_specs=[in_smem] + [whole] * 4,
        out_shape=(
            pltpu.VMEM((chips * SLOT, LANES), jnp.float32),
            pltpu.VMEM((rows, 256), jnp.bfloat16),
        ),
        scratch_shapes=[pltpu.VMEM((chips * CHUNK, LANES), jnp.float32)],
        compiler_params=SMALL,
        name="kernel_gradient",
    )(core, in_vmem(far), in_vmem(g), xt_own, in_vmem(d))
    mine = pl.pallas_call(
        plane_sum_kernel,
        out_shape=pltpu.VMEM((groups * CHUNK, LANES), jnp.float32),
        compiler_params=SMALL,
        name="plane_sum",
    )(in_vmem(exchange_slots(dw).astype(jnp.float32)))
    total = pl.pallas_call(
        lambda p, o: finish_kernel(p, o, scale=scale),
        out_shape=pltpu.VMEM((chips * SLOT, LANES), jnp.float32),
        compiler_params=SMALL,
        name="finish",
    )(exchange(mine, "rep"))
    gathered = exchange_slots(total)
    other = lax.ppermute(gathered, "core", swap)
    dx = pl.pallas_call(
        input_gradient_kernel,
        out_shape=pltpu.VMEM((height, packed), jnp.bfloat16),
        compiler_params=SMALL,
        name="input_gradient",
    )(in_vmem(g_far), in_vmem(g), in_vmem(wt))
    weight_grad, bias_grad, dx = pl.pallas_call(
        unpack_kernel,
        in_specs=[in_smem, whole, whole, whole],
        out_specs=[pl.BlockSpec(memory_space=pltpu.HBM)] * 3,
        out_shape=(
            jax.ShapeDtypeStruct((27, CH, CH), jnp.float32),
            jax.ShapeDtypeStruct((1, CH), jnp.float32),
            jax.ShapeDtypeStruct((height, packed), jnp.bfloat16),
        ),
        scratch_shapes=[
            pltpu.VMEM((chips * CHUNK, LANES), jnp.float32),
            pltpu.VMEM((27, CH, CH), jnp.float32),
            pltpu.VMEM((1, CH), jnp.float32),
            pltpu.SemaphoreType.DMA((6,)),
        ],
        compiler_params=SMALL,
        name="unpack",
    )(core, in_vmem(gathered.astype(jnp.float32)), in_vmem(other.astype(jnp.float32)), in_vmem(dx))
    return dx.reshape(inputs.shape), weight_grad.reshape(3, 3, 3, CH, CH), bias_grad.reshape(CH)


def solution(mesh):
    groups, slabs = mesh.devices.shape
    by_core = jax.sharding.Mesh(mesh.devices.reshape(groups, slabs // 2, 2), ("rep", "chip", "core"))
    split = P("rep", ("chip", "core"), None, None)
    return jax.shard_map(
        on_device,
        mesh=by_core,
        in_specs=(split, split, split, P()),
        out_specs=(split, P(), P()),
        check_vma=False,
    )
```

```python
import jax
import jax.numpy as jnp
from jax import lax
from jax.experimental import pallas as pl
from jax.experimental.pallas import tpu as pltpu
from jax.sharding import PartitionSpec as P


CH = 64
LANES = 2 * CH
SLOT = 16
CHUNK = 14
SMALL = pltpu.CompilerParams(vmem_limit_bytes=16 * 1024 * 1024)


def mask_kernel(preact_ref, grad_ref, x_ref, own_ref, pack_ref, z_ref, dy_ref, sems):
    height, packed = own_ref.shape
    pieces = sems.shape[1]
    columns = [pl.ds(i * (packed // pieces), packed // pieces) for i in range(pieces)]
    loads = [
        (
            pltpu.make_async_copy(preact_ref.at[:, part], z_ref.at[:, part], sems.at[0, i]),
            pltpu.make_async_copy(grad_ref.at[:, part], dy_ref.at[:, part], sems.at[1, i]),
            pltpu.make_async_copy(x_ref.at[:, part], pack_ref.at[height:, part], sems.at[2, i]),
        )
        for i, part in enumerate(columns)
    ]
    for z_load, dy_load, _ in loads:
        z_load.start()
        dy_load.start()
    for _, _, x_load in loads:
        x_load.start()
    for part, (z_load, dy_load, _) in zip(columns, loads):
        z_load.wait()
        dy_load.wait()
        own = jnp.where(z_ref[:, part] > 0, dy_ref[:, part], jnp.zeros((height, packed // pieces), own_ref.dtype))
        own_ref[:, part] = own
        pack_ref[0:height, part] = own
    for _, _, x_load in loads:
        x_load.wait()


def inputs_kernel(pair_ref, xt_ref):
    height, packed = pair_ref.shape[0] // 2, pair_ref.shape[1]
    x_ref = pair_ref.at[height:]
    pairs = packed // LANES
    rows = pairs * height
    x = jnp.concatenate([x_ref[:, LANES * j : LANES * (j + 1)] for j in range(pairs)], axis=0)
    xt = jnp.transpose(x.astype(jnp.float32))
    h = lax.broadcasted_iota(jnp.int32, (LANES, rows), 1) % height
    xt_ref[0:LANES, :] = jnp.where(h == 0, 0.0, pltpu.roll(xt, 1, 1)).astype(jnp.bfloat16)
    xt_ref[LANES : 2 * LANES, :] = xt.astype(jnp.bfloat16)
    xt_ref[2 * LANES :, :] = jnp.where(h == height - 1, 0.0, pltpu.roll(xt, rows - 1, 1)).astype(jnp.bfloat16)


def weights_kernel(core_ref, w_ref, wt_ref):
    core = core_ref[0]
    zero = jnp.zeros((CH, CH), jnp.bfloat16)
    for slot, od in enumerate((2 - 2 * core, 1, 2 * core)):
        for oh in range(3):
            t = 9 * od + 3 * oh
            before, here, after = w_ref[t], w_ref[t + 1], w_ref[t + 2]
            for parity in range(2):
                if parity == 0:
                    parts = (here, before, zero, after)
                else:
                    parts = (after, here, before, zero)
                r = (2 * oh + parity) * CH
                wt_ref[r : r + CH, 256 * slot : 256 * slot + LANES] = jnp.concatenate(parts[:2], axis=1)
                wt_ref[r : r + CH, 256 * slot + LANES : 256 * (slot + 1)] = jnp.concatenate(parts[2:], axis=1)


def lay_out(ref, g_ref, column):
    height, packed = g_ref.shape[0] * LANES // ref.shape[1], ref.shape[1]
    pairs = packed // LANES
    low = lax.broadcasted_iota(jnp.int32, (height, LANES), 1) < CH
    nothing = jnp.zeros((height, LANES), jnp.bfloat16)
    for j in range(pairs):
        at = slice(height * j, height * (j + 1))
        g_ref[at, column : column + LANES] = ref[0:height, LANES * j : LANES * (j + 1)]
        right = ref[0:height, LANES * (j + 1) : LANES * (j + 2)] if j + 1 < pairs else nothing
        left = ref[0:height, LANES * (j - 1) : LANES * j] if j > 0 else nothing
        g_ref[at, column + LANES : column + 256] = jnp.where(low, right, left)


def own_planes_kernel(own_ref, near_ref, xt_own_ref, xt_near_ref, d_ref, g_ref):
    lay_out(own_ref, g_ref, 0)
    lay_out(near_ref, g_ref, 256)
    d = jnp.dot(xt_near_ref[...], g_ref[...], preferred_element_type=jnp.float32)
    own = jnp.dot(xt_own_ref[...], g_ref[:, 0:256], preferred_element_type=jnp.float32)
    d_ref[:, 0:256] = d[:, 0:256]
    d_ref[:, 256:512] = d[:, 256:512] + own


def kernel_gradient_kernel(core_ref, far_ref, g_ref, xt_own_ref, d_ref, slots_ref, g_far_ref, dw_ref):
    lay_out(far_ref, g_far_ref, 0)
    parts = (
        d_ref[:, 0:256] + jnp.dot(xt_own_ref[...], g_far_ref[...], preferred_element_type=jnp.float32),
        d_ref[:, 256:512],
    )
    lo = lax.broadcasted_iota(jnp.int32, (CH, LANES), 1) < CH
    core_0 = jnp.full((CH, LANES), core_ref[0], jnp.int32) == 0

    def block(part, oh, parity, half):
        r = LANES * oh + CH * parity
        return parts[part][r : r + CH, LANES * half : LANES * (half + 1)]

    def swap(v):
        return pltpu.roll(v, CH, 1)

    def two(part, oh):
        return block(part, oh, 0, 0) + jnp.where(lo, swap(block(part, oh, 1, 0)), swap(block(part, oh, 1, 1)))

    def low_one(part, oh):
        return block(part, oh, 1, 0) + swap(block(part, oh, 0, 1))

    def high_one(part, oh):
        return swap(block(part, oh, 1, 0)) + block(part, oh, 0, 1)

    total = jnp.sum(g_ref[:, 0:128].astype(jnp.float32) + g_ref[:, 256:384].astype(jnp.float32), axis=0, keepdims=True)
    first = lax.broadcasted_iota(jnp.int32, (CH, LANES), 0) == 0
    bias = jnp.where(first, jnp.broadcast_to(total + swap(total), (CH, LANES)), 0.0)
    blocks = (
        two(0, 0),
        two(0, 1),
        two(0, 2),
        jnp.where(lo, low_one(0, 0), high_one(0, 1)),
        jnp.where(lo, low_one(0, 2), jnp.where(core_0, high_one(1, 0), high_one(1, 2))),
        jnp.where(core_0, two(1, 0), two(1, 2)),
        jnp.where(core_0, two(1, 1), jnp.where(lo, low_one(1, 1), bias)),
    )
    largest = jnp.max(jnp.abs(blocks[0]), axis=0, keepdims=True)
    for v in blocks[1:]:
        largest = jnp.maximum(largest, jnp.max(jnp.abs(v), axis=0, keepdims=True))
    exponent = exponents(largest)
    unit = jnp.exp2(-exponent)
    for i, v in enumerate(blocks):
        dw_ref[CH * i : CH * (i + 1), :] = v * unit
    for i in range(slots_ref.shape[0] // SLOT):
        slots_ref[SLOT * i : SLOT * (i + 1), :] = to_slot(dw_ref[CHUNK * i : CHUNK * (i + 1), :], exponent)


def input_gradient_kernel(g_far_ref, g_ref, wt_ref, dx_ref):
    height, packed = dx_ref.shape
    pairs = packed // LANES
    rows = pairs * height
    turn = (((1,), (1,)), ((), ()))
    y = lax.dot_general(g_ref[...], wt_ref[:, 256:768], turn, preferred_element_type=jnp.float32)
    y = y + lax.dot_general(g_far_ref[...], wt_ref[:, 0:256], turn, preferred_element_type=jnp.float32)
    h = lax.broadcasted_iota(jnp.int32, (rows, LANES), 0) % height
    up = jnp.where(h == height - 1, 0.0, pltpu.roll(y[:, :LANES], rows - 1, 0))
    down = jnp.where(h == 0, 0.0, pltpu.roll(y[:, 2 * LANES :], 1, 0))
    out = (y[:, LANES : 2 * LANES] + up + down).astype(jnp.bfloat16)
    for j in range(pairs):
        dx_ref[:, LANES * j : LANES * (j + 1)] = out[height * j : height * (j + 1), :]


def exponents(largest):
    return jnp.floor(jnp.log2(jnp.maximum(largest, 1e-30))) - 14.0


def to_slot(rows, exponent):
    return jnp.concatenate([rows, exponent, jnp.zeros((SLOT - CHUNK - 1, LANES), jnp.float32)], axis=0)


def from_slot(slots_ref, i):
    unit = jnp.exp2(slots_ref[SLOT * i + CHUNK : SLOT * i + CHUNK + 1, :])
    return slots_ref[SLOT * i : SLOT * i + CHUNK, :] * unit


def plane_sum_kernel(slots_ref, out_ref):
    sums = [from_slot(slots_ref, i) for i in range(slots_ref.shape[0] // SLOT)]
    while len(sums) > 1:
        sums = [a + b for a, b in zip(sums[::2], sums[1::2], strict=True)]
    for i in range(out_ref.shape[0] // CHUNK):
        out_ref[CHUNK * i : CHUNK * (i + 1), :] = sums[0]


def finish_kernel(parts_ref, out_ref, *, scale):
    s = parts_ref[0:CHUNK, :]
    for i in range(1, parts_ref.shape[0] // CHUNK):
        s = s + parts_ref[CHUNK * i : CHUNK * (i + 1), :]
    s = s * scale
    exponent = exponents(jnp.max(jnp.abs(s), axis=0, keepdims=True))
    slot = to_slot(s * jnp.exp2(-exponent), exponent)
    for i in range(out_ref.shape[0] // SLOT):
        out_ref[SLOT * i : SLOT * (i + 1), :] = slot


def unpack_kernel(
    core_ref, mine_ref, other_ref, dx_ref, weight_ref, bias_ref, dx_out_ref, rows_ref, taps_ref, last_ref, sems
):
    stores = [pltpu.make_async_copy(dx_ref, dx_out_ref, sems.at[0])]
    stores[0].start()
    chips = mine_ref.shape[0] // SLOT
    places = (
        (((19, 18), (22, 21), (25, 24), (20, 23), (26, 11), (10, 9), (13, 12)), ((18, 27), (9, 14))),
        (((1, 0), (4, 3), (7, 6), (2, 5), (8, 17), (16, 15), (14, None)), ((0, 9), (14, 18))),
    )
    core_0 = jnp.full((SLOT, LANES), core_ref[0], jnp.int32) == 0
    for core, (sides, ranges) in enumerate(places):
        for i in range(chips):
            a = mine_ref[SLOT * i : SLOT * (i + 1), :]
            b = other_ref[SLOT * i : SLOT * (i + 1), :]
            v = jnp.where(core_0, a, b) if core == 0 else jnp.where(core_0, b, a)
            rows_ref[CHUNK * i : CHUNK * (i + 1), :] = v[:CHUNK] * jnp.exp2(v[CHUNK : CHUNK + 1])
        for i, (lower, upper) in enumerate(sides):
            v = rows_ref[CH * i : CH * (i + 1), :]
            taps_ref[lower] = v[:, :CH]
            if upper is None:
                last_ref[...] = v[0:1, CH:]
                stores.append(pltpu.make_async_copy(last_ref, bias_ref, sems.at[len(stores)]))
                stores[-1].start()
            else:
                taps_ref[upper] = v[:, CH:]
        for first, end in ranges:
            part = pl.ds(first, end - first)
            stores.append(pltpu.make_async_copy(taps_ref.at[part], weight_ref.at[part], sems.at[len(stores)]))
            stores[-1].start()
    for store in stores:
        store.wait()


def in_vmem(array):
    return pltpu.with_memory_space_constraint(array, pltpu.VMEM)


def in_hbm(array):
    return pltpu.with_memory_space_constraint(array, pltpu.HBM)


def exchange(rows, axis):
    return in_vmem(lax.all_to_all(rows.reshape(-1, 1, LANES), axis, 0, 0, tiled=True).reshape(-1, LANES))


def exchange_slots(slots):
    return lax.all_to_all(slots.astype(jnp.float16), "chip", 0, 0, tiled=True)


def on_device(inputs, preact, grad_out, weight):
    chips = lax.axis_size("chip")
    slabs = chips * lax.axis_size("core")
    groups = lax.axis_size("rep")
    _, planes, height, packed = inputs.shape
    count = inputs.shape[0] * groups * planes * slabs * height * (packed // CH)
    scale = 1.0 / float(count) ** 0.5
    core = lax.axis_index("core").astype(jnp.int32).reshape(1)
    in_smem = pl.BlockSpec(memory_space=pltpu.SMEM)
    whole = pl.BlockSpec(memory_space=pltpu.VMEM)
    rows = height * packed // LANES
    own, pack = pl.pallas_call(
        mask_kernel,
        in_specs=[pl.BlockSpec(memory_space=pltpu.HBM)] * 3,
        out_shape=(
            pltpu.VMEM((height, packed), jnp.bfloat16),
            pltpu.VMEM((2 * height, packed), jnp.bfloat16),
        ),
        scratch_shapes=[pltpu.VMEM((height, packed), jnp.bfloat16)] * 2 + [pltpu.SemaphoreType.DMA((3, 4))],
        compiler_params=SMALL,
        name="mask",
    )(*(in_hbm(a.reshape(height, packed)) for a in (preact, grad_out, inputs)))
    swap = [(0, 1), (1, 0)]
    ends = range(1, slabs - 1, 2)
    far = lax.ppermute(own, ("chip", "core"), [(i, i + 1) for i in ends] + [(i + 1, i) for i in ends])
    near = in_vmem(lax.ppermute(pack, "core", swap))
    wt = pl.pallas_call(
        weights_kernel,
        in_specs=[in_smem, whole],
        out_shape=pltpu.VMEM((3 * LANES, 768), jnp.bfloat16),
        compiler_params=SMALL,
        name="weights",
    )(core, weight.reshape(27, CH, CH))

    def turned(pair):
        return pl.pallas_call(
            inputs_kernel,
            out_shape=pltpu.VMEM((3 * LANES, rows), jnp.bfloat16),
            compiler_params=SMALL,
            name="inputs",
        )(in_vmem(pair))

    xt_own = in_vmem(turned(pack))
    d, g = pl.pallas_call(
        own_planes_kernel,
        out_shape=(
            pltpu.VMEM((3 * LANES, 512), jnp.float32),
            pltpu.VMEM((rows, 512), jnp.bfloat16),
        ),
        compiler_params=SMALL,
        name="own_planes",
    )(in_vmem(own), near, xt_own, in_vmem(turned(near)))
    dw, g_far = pl.pallas_call(
        kernel_gradient_kernel,
        in_specs=[in_smem] + [whole] * 4,
        out_shape=(
            pltpu.VMEM((chips * SLOT, LANES), jnp.float32),
            pltpu.VMEM((rows, 256), jnp.bfloat16),
        ),
        scratch_shapes=[pltpu.VMEM((chips * CHUNK, LANES), jnp.float32)],
        compiler_params=SMALL,
        name="kernel_gradient",
    )(core, in_vmem(far), in_vmem(g), xt_own, in_vmem(d))
    mine = pl.pallas_call(
        plane_sum_kernel,
        out_shape=pltpu.VMEM((groups * CHUNK, LANES), jnp.float32),
        compiler_params=SMALL,
        name="plane_sum",
    )(in_vmem(exchange_slots(dw).astype(jnp.float32)))
    total = pl.pallas_call(
        lambda p, o: finish_kernel(p, o, scale=scale),
        out_shape=pltpu.VMEM((chips * SLOT, LANES), jnp.float32),
        compiler_params=SMALL,
        name="finish",
    )(exchange(mine, "rep"))
    gathered = exchange_slots(total)
    other = lax.ppermute(gathered, "core", swap)
    dx = pl.pallas_call(
        input_gradient_kernel,
        out_shape=pltpu.VMEM((height, packed), jnp.bfloat16),
        compiler_params=SMALL,
        name="input_gradient",
    )(in_vmem(g_far), in_vmem(g), in_vmem(wt))
    weight_grad, bias_grad, dx = pl.pallas_call(
        unpack_kernel,
        in_specs=[in_smem, whole, whole, whole],
        out_specs=[pl.BlockSpec(memory_space=pltpu.HBM)] * 3,
        out_shape=(
            jax.ShapeDtypeStruct((27, CH, CH), jnp.float32),
            jax.ShapeDtypeStruct((1, CH), jnp.float32),
            jax.ShapeDtypeStruct((height, packed), jnp.bfloat16),
        ),
        scratch_shapes=[
            pltpu.VMEM((chips * CHUNK, LANES), jnp.float32),
            pltpu.VMEM((27, CH, CH), jnp.float32),
            pltpu.VMEM((1, CH), jnp.float32),
            pltpu.SemaphoreType.DMA((6,)),
        ],
        compiler_params=SMALL,
        name="unpack",
    )(core, in_vmem(gathered.astype(jnp.float32)), in_vmem(other.astype(jnp.float32)), in_vmem(dx))
    return dx.reshape(inputs.shape), weight_grad.reshape(3, 3, 3, CH, CH), bias_grad.reshape(CH)


def solution(mesh):
    groups, slabs = mesh.devices.shape
    by_core = jax.sharding.Mesh(mesh.devices.reshape(groups, slabs // 2, 2), ("rep", "chip", "core"))
    split = P("rep", ("chip", "core"), None, None)
    return jax.shard_map(
        on_device,
        mesh=by_core,
        in_specs=(split, split, split, P()),
        out_specs=(split, P(), P()),
        check_vma=False,
    )
```

```python
import jax
import jax.numpy as jnp
from jax import lax
from jax.experimental import pallas as pl
from jax.experimental.pallas import tpu as pltpu
from jax.sharding import PartitionSpec as P


CH = 64
LANES = 2 * CH
SLOT = 16
CHUNK = 14
SMALL = pltpu.CompilerParams(vmem_limit_bytes=16 * 1024 * 1024)


def mask_kernel(preact_ref, grad_ref, x_ref, own_ref, pack_ref, z_ref, dy_ref, sems):
    height = own_ref.shape[0]
    loads = (
        pltpu.make_async_copy(preact_ref, z_ref, sems.at[0]),
        pltpu.make_async_copy(grad_ref, dy_ref, sems.at[1]),
        pltpu.make_async_copy(x_ref, pack_ref.at[height:], sems.at[2]),
    )
    for load in loads:
        load.start()
    loads[0].wait()
    loads[1].wait()
    own = jnp.where(z_ref[...] > 0, dy_ref[...], jnp.zeros_like(dy_ref))
    own_ref[...] = own
    pack_ref[0:height, :] = own
    loads[2].wait()


def inputs_kernel(pair_ref, xt_ref):
    height, packed = pair_ref.shape[0] // 2, pair_ref.shape[1]
    x_ref = pair_ref.at[height:]
    pairs = packed // LANES
    rows = pairs * height
    x = jnp.concatenate([x_ref[:, LANES * j : LANES * (j + 1)] for j in range(pairs)], axis=0)
    xt = jnp.transpose(x.astype(jnp.float32))
    h = lax.broadcasted_iota(jnp.int32, (LANES, rows), 1) % height
    xt_ref[0:LANES, :] = jnp.where(h == 0, 0.0, pltpu.roll(xt, 1, 1)).astype(jnp.bfloat16)
    xt_ref[LANES : 2 * LANES, :] = xt.astype(jnp.bfloat16)
    xt_ref[2 * LANES :, :] = jnp.where(h == height - 1, 0.0, pltpu.roll(xt, rows - 1, 1)).astype(jnp.bfloat16)


def weights_kernel(core_ref, w_ref, wt_ref):
    core = core_ref[0]
    zero = jnp.zeros((CH, CH), jnp.bfloat16)
    for slot, od in enumerate((2 - 2 * core, 1, 2 * core)):
        for oh in range(3):
            t = 9 * od + 3 * oh
            before, here, after = w_ref[t], w_ref[t + 1], w_ref[t + 2]
            for parity in range(2):
                if parity == 0:
                    parts = (here, before, zero, after)
                else:
                    parts = (after, here, before, zero)
                r = (2 * oh + parity) * CH
                wt_ref[r : r + CH, 256 * slot : 256 * slot + LANES] = jnp.concatenate(parts[:2], axis=1)
                wt_ref[r : r + CH, 256 * slot + LANES : 256 * (slot + 1)] = jnp.concatenate(parts[2:], axis=1)


def lay_out(ref, g_ref, column):
    height, packed = g_ref.shape[0] * LANES // ref.shape[1], ref.shape[1]
    pairs = packed // LANES
    low = lax.broadcasted_iota(jnp.int32, (height, LANES), 1) < CH
    nothing = jnp.zeros((height, LANES), jnp.bfloat16)
    for j in range(pairs):
        at = slice(height * j, height * (j + 1))
        g_ref[at, column : column + LANES] = ref[0:height, LANES * j : LANES * (j + 1)]
        right = ref[0:height, LANES * (j + 1) : LANES * (j + 2)] if j + 1 < pairs else nothing
        left = ref[0:height, LANES * (j - 1) : LANES * j] if j > 0 else nothing
        g_ref[at, column + LANES : column + 256] = jnp.where(low, right, left)


def own_planes_kernel(own_ref, near_ref, xt_own_ref, xt_near_ref, d_ref, g_ref):
    lay_out(own_ref, g_ref, 0)
    lay_out(near_ref, g_ref, 256)
    d = jnp.dot(xt_near_ref[...], g_ref[...], preferred_element_type=jnp.float32)
    own = jnp.dot(xt_own_ref[...], g_ref[:, 0:256], preferred_element_type=jnp.float32)
    d_ref[:, 0:256] = d[:, 0:256]
    d_ref[:, 256:512] = d[:, 256:512] + own


def kernel_gradient_kernel(core_ref, far_ref, g_ref, xt_own_ref, d_ref, slots_ref, g_far_ref, dw_ref):
    lay_out(far_ref, g_far_ref, 0)
    parts = (
        d_ref[:, 0:256] + jnp.dot(xt_own_ref[...], g_far_ref[...], preferred_element_type=jnp.float32),
        d_ref[:, 256:512],
    )
    lo = lax.broadcasted_iota(jnp.int32, (CH, LANES), 1) < CH
    core_0 = jnp.full((CH, LANES), core_ref[0], jnp.int32) == 0

    def block(part, oh, parity, half):
        r = LANES * oh + CH * parity
        return parts[part][r : r + CH, LANES * half : LANES * (half + 1)]

    def swap(v):
        return pltpu.roll(v, CH, 1)

    def two(part, oh):
        return block(part, oh, 0, 0) + jnp.where(lo, swap(block(part, oh, 1, 0)), swap(block(part, oh, 1, 1)))

    def low_one(part, oh):
        return block(part, oh, 1, 0) + swap(block(part, oh, 0, 1))

    def high_one(part, oh):
        return swap(block(part, oh, 1, 0)) + block(part, oh, 0, 1)

    total = jnp.sum(g_ref[:, 0:128].astype(jnp.float32) + g_ref[:, 256:384].astype(jnp.float32), axis=0, keepdims=True)
    first = lax.broadcasted_iota(jnp.int32, (CH, LANES), 0) == 0
    bias = jnp.where(first, jnp.broadcast_to(total + swap(total), (CH, LANES)), 0.0)
    blocks = (
        two(0, 0),
        two(0, 1),
        two(0, 2),
        jnp.where(lo, low_one(0, 0), high_one(0, 1)),
        jnp.where(lo, low_one(0, 2), jnp.where(core_0, high_one(1, 0), high_one(1, 2))),
        jnp.where(core_0, two(1, 0), two(1, 2)),
        jnp.where(core_0, two(1, 1), jnp.where(lo, low_one(1, 1), bias)),
    )
    largest = jnp.max(jnp.abs(blocks[0]), axis=0, keepdims=True)
    for v in blocks[1:]:
        largest = jnp.maximum(largest, jnp.max(jnp.abs(v), axis=0, keepdims=True))
    exponent = exponents(largest)
    unit = jnp.exp2(-exponent)
    for i, v in enumerate(blocks):
        dw_ref[CH * i : CH * (i + 1), :] = v * unit
    for i in range(slots_ref.shape[0] // SLOT):
        slots_ref[SLOT * i : SLOT * (i + 1), :] = to_slot(dw_ref[CHUNK * i : CHUNK * (i + 1), :], exponent)


def input_gradient_kernel(g_far_ref, g_ref, wt_ref, dx_ref):
    height, packed = dx_ref.shape
    pairs = packed // LANES
    rows = pairs * height
    turn = (((1,), (1,)), ((), ()))
    y = lax.dot_general(g_ref[...], wt_ref[:, 256:768], turn, preferred_element_type=jnp.float32)
    y = y + lax.dot_general(g_far_ref[...], wt_ref[:, 0:256], turn, preferred_element_type=jnp.float32)
    h = lax.broadcasted_iota(jnp.int32, (rows, LANES), 0) % height
    up = jnp.where(h == height - 1, 0.0, pltpu.roll(y[:, :LANES], rows - 1, 0))
    down = jnp.where(h == 0, 0.0, pltpu.roll(y[:, 2 * LANES :], 1, 0))
    out = (y[:, LANES : 2 * LANES] + up + down).astype(jnp.bfloat16)
    for j in range(pairs):
        dx_ref[:, LANES * j : LANES * (j + 1)] = out[height * j : height * (j + 1), :]


def exponents(largest):
    return jnp.floor(jnp.log2(jnp.maximum(largest, 1e-30))) - 14.0


def to_slot(rows, exponent):
    return jnp.concatenate([rows, exponent, jnp.zeros((SLOT - CHUNK - 1, LANES), jnp.float32)], axis=0)


def from_slot(slots_ref, i):
    unit = jnp.exp2(slots_ref[SLOT * i + CHUNK : SLOT * i + CHUNK + 1, :])
    return slots_ref[SLOT * i : SLOT * i + CHUNK, :] * unit


def plane_sum_kernel(slots_ref, out_ref):
    sums = [from_slot(slots_ref, i) for i in range(slots_ref.shape[0] // SLOT)]
    while len(sums) > 1:
        sums = [a + b for a, b in zip(sums[::2], sums[1::2], strict=True)]
    for i in range(out_ref.shape[0] // CHUNK):
        out_ref[CHUNK * i : CHUNK * (i + 1), :] = sums[0]


def finish_kernel(parts_ref, out_ref, *, scale):
    s = parts_ref[0:CHUNK, :]
    for i in range(1, parts_ref.shape[0] // CHUNK):
        s = s + parts_ref[CHUNK * i : CHUNK * (i + 1), :]
    s = s * scale
    exponent = exponents(jnp.max(jnp.abs(s), axis=0, keepdims=True))
    slot = to_slot(s * jnp.exp2(-exponent), exponent)
    for i in range(out_ref.shape[0] // SLOT):
        out_ref[SLOT * i : SLOT * (i + 1), :] = slot


def unpack_kernel(
    slots_ref, dx_ref, weight_ref, bias_ref, dx_out_ref, rows_ref, taps_ref, last_ref, sems
):
    stores = [pltpu.make_async_copy(dx_ref, dx_out_ref, sems.at[0])]
    stores[0].start()
    chips = slots_ref.shape[0] // (2 * SLOT)
    places = (
        (((19, 18), (22, 21), (25, 24), (20, 23), (26, 11), (10, 9), (13, 12)), ((18, 27), (9, 14))),
        (((1, 0), (4, 3), (7, 6), (2, 5), (8, 17), (16, 15), (14, None)), ((0, 9), (14, 18))),
    )
    for core, (sides, ranges) in enumerate(places):
        for i in range(chips):
            rows_ref[CHUNK * i : CHUNK * (i + 1), :] = from_slot(slots_ref, 2 * i + core)
        for i, (lower, upper) in enumerate(sides):
            v = rows_ref[CH * i : CH * (i + 1), :]
            taps_ref[lower] = v[:, :CH]
            if upper is None:
                last_ref[...] = v[0:1, CH:]
                stores.append(pltpu.make_async_copy(last_ref, bias_ref, sems.at[len(stores)]))
                stores[-1].start()
            else:
                taps_ref[upper] = v[:, CH:]
        for first, end in ranges:
            part = pl.ds(first, end - first)
            stores.append(pltpu.make_async_copy(taps_ref.at[part], weight_ref.at[part], sems.at[len(stores)]))
            stores[-1].start()
    for store in stores:
        store.wait()


def in_vmem(array):
    return pltpu.with_memory_space_constraint(array, pltpu.VMEM)


def in_hbm(array):
    return pltpu.with_memory_space_constraint(array, pltpu.HBM)


def exchange(rows, axis):
    return in_vmem(lax.all_to_all(rows.reshape(-1, 1, LANES), axis, 0, 0, tiled=True).reshape(-1, LANES))


def exchange_slots(slots, axis):
    return lax.all_to_all(slots.astype(jnp.float16), axis, 0, 0, tiled=True)


def on_device(inputs, preact, grad_out, weight):
    chips = lax.axis_size("chip")
    slabs = chips * lax.axis_size("core")
    groups = lax.axis_size("rep")
    _, planes, height, packed = inputs.shape
    count = inputs.shape[0] * groups * planes * slabs * height * (packed // CH)
    scale = 1.0 / float(count) ** 0.5
    core = lax.axis_index("core").astype(jnp.int32).reshape(1)
    in_smem = pl.BlockSpec(memory_space=pltpu.SMEM)
    whole = pl.BlockSpec(memory_space=pltpu.VMEM)
    rows = height * packed // LANES
    own, pack = pl.pallas_call(
        mask_kernel,
        in_specs=[pl.BlockSpec(memory_space=pltpu.HBM)] * 3,
        out_shape=(
            pltpu.VMEM((height, packed), jnp.bfloat16),
            pltpu.VMEM((2 * height, packed), jnp.bfloat16),
        ),
        scratch_shapes=[pltpu.VMEM((height, packed), jnp.bfloat16)] * 2 + [pltpu.SemaphoreType.DMA((3,))],
        compiler_params=SMALL,
        name="mask",
    )(*(in_hbm(a.reshape(height, packed)) for a in (preact, grad_out, inputs)))
    swap = [(0, 1), (1, 0)]
    ends = range(1, slabs - 1, 2)
    far = lax.ppermute(own, ("chip", "core"), [(i, i + 1) for i in ends] + [(i + 1, i) for i in ends])
    near = in_vmem(lax.ppermute(pack, "core", swap))
    wt = pl.pallas_call(
        weights_kernel,
        in_specs=[in_smem, whole],
        out_shape=pltpu.VMEM((3 * LANES, 768), jnp.bfloat16),
        compiler_params=SMALL,
        name="weights",
    )(core, weight.reshape(27, CH, CH))

    def turned(pair):
        return pl.pallas_call(
            inputs_kernel,
            out_shape=pltpu.VMEM((3 * LANES, rows), jnp.bfloat16),
            compiler_params=SMALL,
            name="inputs",
        )(in_vmem(pair))

    xt_own = in_vmem(turned(pack))
    d, g = pl.pallas_call(
        own_planes_kernel,
        out_shape=(
            pltpu.VMEM((3 * LANES, 512), jnp.float32),
            pltpu.VMEM((rows, 512), jnp.bfloat16),
        ),
        compiler_params=SMALL,
        name="own_planes",
    )(in_vmem(own), near, xt_own, in_vmem(turned(near)))
    dw, g_far = pl.pallas_call(
        kernel_gradient_kernel,
        in_specs=[in_smem] + [whole] * 4,
        out_shape=(
            pltpu.VMEM((chips * SLOT, LANES), jnp.float32),
            pltpu.VMEM((rows, 256), jnp.bfloat16),
        ),
        scratch_shapes=[pltpu.VMEM((chips * CHUNK, LANES), jnp.float32)],
        compiler_params=SMALL,
        name="kernel_gradient",
    )(core, in_vmem(far), in_vmem(g), xt_own, in_vmem(d))
    mine = pl.pallas_call(
        plane_sum_kernel,
        out_shape=pltpu.VMEM((groups * CHUNK, LANES), jnp.float32),
        compiler_params=SMALL,
        name="plane_sum",
    )(in_vmem(exchange_slots(dw, "chip").astype(jnp.float32)))
    summed = exchange(mine, "rep")
    dx = pl.pallas_call(
        input_gradient_kernel,
        out_shape=pltpu.VMEM((height, packed), jnp.bfloat16),
        compiler_params=SMALL,
        name="input_gradient",
    )(in_vmem(g_far), in_vmem(g), in_vmem(wt))
    total = pl.pallas_call(
        lambda p, o: finish_kernel(p, o, scale=scale),
        out_shape=pltpu.VMEM((slabs * SLOT, LANES), jnp.float32),
        compiler_params=SMALL,
        name="finish",
    )(summed)
    gathered = exchange_slots(total, ("chip", "core"))
    weight_grad, bias_grad, dx = pl.pallas_call(
        unpack_kernel,
        in_specs=[whole, whole],
        out_specs=[pl.BlockSpec(memory_space=pltpu.HBM)] * 3,
        out_shape=(
            jax.ShapeDtypeStruct((27, CH, CH), jnp.float32),
            jax.ShapeDtypeStruct((1, CH), jnp.float32),
            jax.ShapeDtypeStruct((height, packed), jnp.bfloat16),
        ),
        scratch_shapes=[
            pltpu.VMEM((chips * CHUNK, LANES), jnp.float32),
            pltpu.VMEM((27, CH, CH), jnp.float32),
            pltpu.VMEM((1, CH), jnp.float32),
            pltpu.SemaphoreType.DMA((6,)),
        ],
        compiler_params=SMALL,
        name="unpack",
    )(in_vmem(gathered.astype(jnp.float32)), in_vmem(dx))
    return dx.reshape(inputs.shape), weight_grad.reshape(3, 3, 3, CH, CH), bias_grad.reshape(CH)


def solution(mesh):
    groups, slabs = mesh.devices.shape
    by_core = jax.sharding.Mesh(mesh.devices.reshape(groups, slabs // 2, 2), ("rep", "chip", "core"))
    split = P("rep", ("chip", "core"), None, None)
    return jax.shard_map(
        on_device,
        mesh=by_core,
        in_specs=(split, split, split, P()),
        out_specs=(split, P(), P()),
        check_vma=False,
    )
```
